32 devices in a mesh: grp: 2 (over y), depth: 4 (over z), rows: 4 (over x, core).
Axes of the slice: x: 2, y: 2, z: 4, core: 2. Of those that a mesh axis runs over, the one named last changes fastest.
Arguments:
- volume: bfloat16 [16, 64, 256, 128], P(('grp', 'depth'), None, 'rows'), parts along dimension 0, may hold values from -6 to 6
- conv_one: bfloat16 [3, 3, 128, 128], replicated, may hold values from -0.1875 to 0.1875
- bias_one: float32 [128], replicated, may hold values from -3 to 3
- conv_two: bfloat16 [3, 3, 128, 128], replicated, may hold values from -0.1875 to 0.1875
- bias_two: float32 [128], replicated, may hold values from -3 to 3
- opacity_weight: float32 [128], replicated, may hold values from -0.5 to 0.5
- opacity_bias: float32 [8], P('depth'), may hold values from -5 to -2.5
Outputs:
- image: float32 [128, 256, 128], P(('grp', 'depth'), 'rows'), parts along dimension 0
The draws below stay inside these ranges and needn't reach their ends.
There are 2 independent parts, one for each index of `grp`. The reference program is written for one: setup_inputs(seed, part) draws one part's arguments, and reference() takes and returns one part's arrays. A program takes and returns all parts, laid end to end along the dimension named above; an argument that names none is the same for every part. Nothing has to cross between parts.
All inputs are finite; a program needn't handle non-finite values.
Results may differ from the reference program's by a relative error of at most 0.0016.
Values may be sent and summed in bfloat16 or wider, within the bound.
No kernel may reach another device: no remote copies, remote signals or barrier semaphores. Data moves between devices by JAX's collectives and lax.ppermute only.
A program may use at most 64 MiB of HBM per device.

```python
import jax
import jax.numpy as jnp
from jax import lax

C = 128
W = 64
DEPTHS = 8
H = 256


def block_scale(key, shape, pieces, low, top_value):
    def one(dim, blocks):
        steps = jax.random.uniform(jax.random.fold_in(jax.random.fold_in(key, 6), dim), (blocks,), jnp.float32, low / len(pieces), top_value / len(pieces))
        return jnp.repeat(jnp.exp(steps), shape[dim] // blocks).reshape((-1,) + (1,) * (len(shape) - dim - 1))

    loudness = one(*pieces[0])
    for cut in pieces[1:]:
        loudness = loudness * one(*cut)
    return loudness


def scatter_about(stream_key, extent, deviation, most, pieces=(), kind=jnp.bfloat16):
    drawn = jax.random.normal(stream_key, extent, jnp.float32) * deviation
    if len(pieces) > 0:
        drawn = block_scale(stream_key, extent, pieces, -0.22, 0.18) * drawn
    return jnp.clip(drawn, min=-most, max=most).astype(kind)


def setup_inputs(seed: int = 0, part: int = 0) -> dict:
    splits = jax.random.split(jax.random.key(seed), 8)
    part_keys = jax.random.split(jax.random.fold_in(splits[7], part), 8)
    return {
        "volume": scatter_about(part_keys[0], (DEPTHS, W, H, C), 1.0, 6.0, ((0, 4), (2, 4))),
        "conv_one": scatter_about(splits[1], (3, 3, C, C), (9 * C) ** -0.5, 0.1875),
        "bias_one": scatter_about(splits[2], (C,), 0.5, 3.0, (), jnp.float32),
        "conv_two": scatter_about(splits[3], (3, 3, C, C), (9 * C) ** -0.5, 0.1875),
        "bias_two": scatter_about(splits[4], (C,), 0.5, 3.0, (), jnp.float32),
        "opacity_weight": scatter_about(splits[5], (C,), C ** -0.5, 0.5, (), jnp.float32),
        "opacity_bias": jnp.clip(-5.0 + 2.5 * jax.random.uniform(splits[6], (DEPTHS,), jnp.float32) ** block_scale(splits[6], (DEPTHS,), ((0, 4),), -0.2, 0.2), -5.0, -2.5),
    }


def convolve(plane, kernel, bias):
    out = lax.conv_general_dilated(plane[None], kernel, (1, 1), ((1, 1), (1, 1)), dimension_numbers=("NHWC", "HWIO", "NHWC"), preferred_element_type=jnp.float32)
    return out[0] + bias


def reference(volume, conv_one, bias_one, conv_two, bias_two, opacity_weight, opacity_bias):
    def step(carry, inputs):
        color, trans = carry
        plane, offset = inputs
        hidden = jax.nn.gelu(convolve(plane, conv_one, bias_one)).astype(jnp.bfloat16)
        features = jax.nn.gelu(convolve(hidden, conv_two, bias_two))
        alpha = jax.nn.sigmoid(jnp.sum(features * opacity_weight, axis=-1) + offset)
        color = color + (trans * alpha)[..., None] * features
        trans = trans * (1.0 - alpha)
        return (color, trans), None

    start = (jnp.zeros((W, H, C), jnp.float32), jnp.ones((W, H), jnp.float32))
    (color, trans), unused = lax.scan(step, start, (volume, opacity_bias))
    return color
```

```python
import functools

import jax
import jax.numpy as jnp
from jax import lax
from jax.experimental import pallas as pl
from jax.experimental.pallas import tpu as pltpu
from jax.sharding import PartitionSpec as P

VM = pl.BlockSpec(memory_space=pltpu.VMEM)
ANY = pl.BlockSpec(memory_space=pl.ANY)
F32 = jnp.float32
BF16 = jnp.bfloat16


def gelu(x):
    c = 0.7978845608028654
    half = 0.5 * x
    return half + half * jnp.tanh(x * (c + (c * 0.044715) * (x * x)))


def pair_weights(w_ref):
    zero = jnp.zeros((w_ref.shape[2], w_ref.shape[3]), w_ref.dtype)
    blocks = []
    for j in range(4):
        for d in range(3):
            first = w_ref[j, d] if j < 3 else zero
            second = w_ref[j - 1, d] if j > 0 else zero
            blocks.append(jnp.concatenate([first, second], axis=1))
    return jnp.concatenate(blocks, axis=0)


def edges_kernel(x_hbm, top_ref, bot_ref, buf, sem):
    rows = x_hbm.shape[2]
    a = pltpu.make_async_copy(x_hbm.at[:, :, pl.ds(0, 8)], buf.at[0], sem.at[0])
    b = pltpu.make_async_copy(x_hbm.at[:, :, pl.ds(rows - 8, 8)], buf.at[1], sem.at[1])
    a.start()
    b.start()
    a.wait()
    top_ref[...] = buf[0, :, :, 0:2]
    b.wait()
    bot_ref[...] = buf[1, :, :, 6:8]


def edges(x):
    planes, cols, rows, ch = x.shape
    shape = jax.ShapeDtypeStruct((planes, cols, 2, ch), x.dtype)
    return pl.pallas_call(
        edges_kernel,
        out_shape=(shape, shape),
        in_specs=[ANY],
        out_specs=(VM, VM),
        scratch_shapes=[
            pltpu.VMEM((2, planes, cols, 8, ch), x.dtype),
            pltpu.SemaphoreType.DMA((2,)),
        ],
        compiler_params=pltpu.CompilerParams(vmem_limit_bytes=8 << 20),
    )(x)


def chunk_kernel(pick, packed, x_ref, above_ref, below_ref, w1_ref, w2_ref, par_ref, *refs):
    if packed:
        out_ref, f_ref, xs, f2_ref, hs, fs = refs
    else:
        out_ref, trans_ref, f_ref, xs, f2_ref, hs, fs = refs
    planes, cols, rows, ch = x_ref.shape
    ext = rows + 16
    nc = fs.shape[1]
    slots = f_ref.shape[0]
    c0 = pick() * nc
    for i in range(planes * (nc + 4)):
        p, c = divmod(i, nc + 4)
        at = c0 - 2 + c
        inside = jnp.logical_and(at >= 0, at < cols)
        at = jnp.clip(at, 0, cols - 1)
        keep = jnp.where(inside, 1.0, 0.0)
        f = f_ref.at[i % slots]
        f[16 : 16 + rows] = x_ref[p, at].astype(F32) * keep
        f[14:16] = above_ref[p, at].astype(F32) * keep
        f[16 + rows : 18 + rows] = below_ref[p, at].astype(F32) * keep
        for d in range(3):
            xs[d, p, c] = f[7 + d : 7 + d + ext].astype(BF16)
    here = lax.axis_index("rows")
    above = jnp.where(here == 0, 0.0, 1.0)
    below = jnp.where(here == lax.axis_size("rows") - 1, 0.0, 1.0)
    bias_one = par_ref[0:1]
    bias_two = par_ref[1:2]
    opacity = par_ref[2:3]
    weights = pair_weights(w1_ref)
    for p in range(planes):
        taps = []
        for j in range(4):
            for d in range(3):
                taps.append(jnp.concatenate([xs[d, p, g + j] for g in range(0, nc + 2, 2)], axis=0))
        y = jnp.dot(jnp.concatenate(taps, axis=1), weights, preferred_element_type=F32)
        for c in range(nc + 2):
            g, o = divmod(c, 2)
            v = gelu(y[g * ext : (g + 1) * ext, o * ch : (o + 1) * ch] + bias_one)
            if c == 0:
                v = v * jnp.where(c0 > 0, 1.0, 0.0)
            if c == nc + 1:
                v = v * jnp.where(c0 + nc < cols, 1.0, 0.0)
            f2 = f2_ref.at[p, c]
            f2[...] = v
            f2[7:8] = f2[7:8] * above
            f2[8 + rows : 9 + rows] = f2[8 + rows : 9 + rows] * below
            for d in range(3):
                hs[d, p, c] = f2[7 + d : 7 + d + rows].astype(BF16)
    lane = lax.broadcasted_iota(jnp.int32, (rows, ch), 1)
    weights = pair_weights(w2_ref)
    logits = [jnp.zeros((rows, ch), F32) for _ in range(planes)]
    taps = []
    for j in range(4):
        for d in range(3):
            taps.append(
                jnp.concatenate(
                    [hs[d, p, g + j] for g in range(0, nc, 2) for p in range(planes)], axis=0
                )
            )
    y = jnp.dot(jnp.concatenate(taps, axis=1), weights, preferred_element_type=F32)
    for c in range(nc):
        g, o = divmod(c, 2)
        for p in range(planes):
            r0 = (g * planes + p) * rows
            f = gelu(y[r0 : r0 + rows, o * ch : (o + 1) * ch] + bias_two)
            total = jnp.sum(f * opacity, axis=1, keepdims=True)
            logits[p] = jnp.where(lane == c, total, logits[p])
            fs[p, c] = f
    parts = []
    trans = None
    for p in range(planes):
        alpha = 1.0 / (1.0 + jnp.exp(-(logits[p] + par_ref[3 + p : 4 + p])))
        if p == 0:
            parts.append(alpha)
            trans = 1.0 - alpha
        else:
            parts.append(trans * alpha)
            trans = trans * (1.0 - alpha)
    for c in range(nc):
        color = sum(parts[p][:, c : c + 1] * fs[p, c] for p in range(planes))
        out_ref[c] = color.astype(out_ref.dtype)
    if packed:
        high = trans.astype(BF16).astype(F32)
        low = pltpu.roll(trans - high, nc, axis=1)
        out_ref[nc] = jnp.where(lane < nc, high, low).astype(out_ref.dtype)
    else:
        trans_ref[...] = trans


def chunk(pick, nc, packed, x, above, below, w1, w2, par):
    planes, cols, rows, ch = x.shape
    ext = rows + 16
    if packed:
        out_shape = jax.ShapeDtypeStruct((nc + 1, rows, ch), BF16)
        out_specs = VM
    else:
        out_shape = (
            jax.ShapeDtypeStruct((nc, rows, ch), F32),
            jax.ShapeDtypeStruct((rows, ch), F32),
        )
        out_specs = (VM, VM)
    return pl.pallas_call(
        functools.partial(chunk_kernel, pick, packed),
        out_shape=out_shape,
        in_specs=[VM] * 6,
        out_specs=out_specs,
        scratch_shapes=[
            pltpu.VMEM((8, rows + 32, ch), F32),
            pltpu.VMEM((3, planes, nc + 4, ext, ch), BF16),
            pltpu.VMEM((planes, nc + 2, ext, ch), F32),
            pltpu.VMEM((3, planes, nc + 2, rows, ch), BF16),
            pltpu.VMEM((planes, nc, rows, ch), F32),
        ],
        compiler_params=pltpu.CompilerParams(vmem_limit_bytes=16 << 20),
    )(x, above, below, w1, w2, par)


def combine_kernel(own_ref, trans_ref, *refs):
    *got_refs, out_ref = refs
    nc, rows, ch = own_ref.shape
    here = lax.axis_index("depth")
    trans = [trans_ref[...]]
    for ref in got_refs:
        t = ref[nc].astype(F32)
        trans.append(t + pltpu.roll(t, ch - nc, axis=1))
    scale = []
    for k in range(len(trans)):
        w = None
        for m in range(len(trans)):
            if m != k:
                front = jnp.bitwise_xor(here, m) < jnp.bitwise_xor(here, k)
                term = jnp.where(front, trans[m], 1.0)
                w = term if w is None else w * term
        scale.append(w)
    for c in range(nc):
        total = scale[0][:, c : c + 1] * own_ref[c]
        for k, ref in enumerate(got_refs):
            total = total + scale[k + 1][:, c : c + 1] * ref[c].astype(F32)
        out_ref[c] = total


def combine(own, trans, got):
    return pl.pallas_call(
        combine_kernel,
        out_shape=jax.ShapeDtypeStruct(own.shape, F32),
        in_specs=[VM] * (2 + len(got)),
        out_specs=VM,
        compiler_params=pltpu.CompilerParams(vmem_limit_bytes=8 << 20),
    )(own, trans, *got)


def exchange(value, axis, mask):
    pairs = [(i, i ^ mask) for i in range(lax.axis_size(axis))]
    return lax.ppermute(value, axis, pairs)


def pick_half(array, remaining, bit_set):
    shaped = array.reshape((remaining // 2, 2, -1) + array.shape[1:])
    first_half = shaped[:, 0].reshape((-1,) + array.shape[1:])
    second_half = shaped[:, 1].reshape((-1,) + array.shape[1:])
    keep = jnp.where(bit_set, second_half, first_half)
    other = jnp.where(bit_set, first_half, second_half)
    return (keep, other)


def butterfly(color, trans):
    position = lax.axis_index("depth")
    slabs = lax.axis_size("depth")
    for level in range(slabs.bit_length() - 1):
        remaining = slabs >> level
        bit_set = jnp.right_shift(position, level) % 2 == 1
        keep_color, send_color = pick_half(color, remaining, bit_set)
        keep_trans, send_trans = pick_half(trans, remaining, bit_set)
        got_color = exchange(send_color, "depth", 2**level)
        got_trans = exchange(send_trans, "depth", 2**level)
        color = jnp.where(
            bit_set,
            got_color + got_trans[..., None] * keep_color,
            keep_color + keep_trans[..., None] * got_color,
        )
        trans = keep_trans * got_trans
    return color


def per_device(volume, conv_one, bias_one, conv_two, bias_two, opacity_weight, opacity_bias):
    planes, cols, rows, ch = volume.shape
    slabs = lax.axis_size("depth")
    size = lax.axis_size("rows")
    par = jnp.concatenate(
        [
            jnp.stack([bias_one, bias_two, opacity_weight]),
            jnp.broadcast_to(opacity_bias[:, None], (planes, ch)),
        ]
    )
    top, bot = edges(volume)
    above = lax.ppermute(bot, "rows", [(i, i + 1) for i in range(size - 1)])
    below = lax.ppermute(top, "rows", [(i + 1, i) for i in range(size - 1)])
    args = (volume, above, below, conv_one, conv_two, par)
    if slabs > 4:
        nc = 16
        done = [
            chunk(functools.partial(jnp.int32, i), nc, False, *args) for i in range(cols // nc)
        ]
        color = jnp.concatenate([c for c, _ in done])
        trans = jnp.concatenate([jnp.transpose(t[:, :nc]) for _, t in done])
        return butterfly(color, trans)
    nc = cols // slabs

    def pick(k):
        return lambda: jnp.bitwise_xor(lax.axis_index("depth"), k)

    got = {}
    for k in [k for k in (2, 3, 1) if k < slabs]:
        got[k] = exchange(chunk(pick(k), nc, True, *args), "depth", k)
    own, trans = chunk(pick(0), nc, False, *args)
    return combine(own, trans, [got[k] for k in sorted(got)])


def solution(mesh):
    in_specs = (P(("grp", "depth"), None, "rows", None), P(), P(), P(), P(), P(), P("depth"))
    out_specs = P(("grp", "depth"), "rows", None)
    return jax.shard_map(
        per_device, mesh=mesh, in_specs=in_specs, out_specs=out_specs, check_vma=False
    )
```

```python
import functools

import jax
import jax.numpy as jnp
from jax import lax
from jax.experimental import pallas as pl
from jax.experimental.pallas import tpu as pltpu
from jax.sharding import PartitionSpec as P

VM = pl.BlockSpec(memory_space=pltpu.VMEM)
HBM = pl.BlockSpec(memory_space=pltpu.HBM)
F32 = jnp.float32
BF16 = jnp.bfloat16


def gelu(x):
    c = 0.7978845608028654
    half = 0.5 * x
    return half + half * jnp.tanh(x * (c + (c * 0.044715) * (x * x)))


def pair_weights(w_ref):
    zero = jnp.zeros((w_ref.shape[2], w_ref.shape[3]), w_ref.dtype)
    blocks = []
    for j in range(4):
        for d in range(3):
            first = w_ref[j, d] if j < 3 else zero
            second = w_ref[j - 1, d] if j > 0 else zero
            blocks.append(jnp.concatenate([first, second], axis=1))
    return jnp.concatenate(blocks, axis=0)


def edges_kernel(x_hbm, top_ref, bot_ref, buf, sem):
    rows = x_hbm.shape[2]
    a = pltpu.make_async_copy(x_hbm.at[:, :, pl.ds(0, 8)], buf.at[0], sem.at[0])
    b = pltpu.make_async_copy(x_hbm.at[:, :, pl.ds(rows - 8, 8)], buf.at[1], sem.at[1])
    a.start()
    b.start()
    a.wait()
    top_ref[...] = buf[0, :, :, 0:2]
    b.wait()
    bot_ref[...] = buf[1, :, :, 6:8]


def edges(x):
    planes, cols, rows, ch = x.shape
    shape = jax.ShapeDtypeStruct((planes, cols, 2, ch), x.dtype)
    return pl.pallas_call(
        edges_kernel,
        out_shape=(shape, shape),
        in_specs=[HBM],
        out_specs=(VM, VM),
        scratch_shapes=[
            pltpu.VMEM((2, planes, cols, 8, ch), x.dtype),
            pltpu.SemaphoreType.DMA((2,)),
        ],
        compiler_params=pltpu.CompilerParams(vmem_limit_bytes=8 << 20),
    )(x)


def load_shifted(part, x_ref, p, at, keep, f, xs, c, halo):
    rows = x_ref.shape[2]
    if part == "strips":
        above_ref, below_ref = halo
        f[8:24] = x_ref[p, at, 0:16].astype(F32) * keep
        f[6:8] = above_ref[p, at].astype(F32) * keep
        f[40:56] = x_ref[p, at, rows - 16 : rows].astype(F32) * keep
        f[56:58] = below_ref[p, at].astype(F32) * keep
        for d in range(3):
            xs[d, p, c, 0:16] = f[3 + d : 19 + d].astype(BF16)
            xs[d, p, c, 16:32] = f[43 + d : 59 + d].astype(BF16)
        return
    lead = 8 if part == "whole" else 0
    f[16 : 16 + rows] = x_ref[p, at].astype(F32) * keep
    if part == "whole":
        above_ref, below_ref = halo
        f[14:16] = above_ref[p, at].astype(F32) * keep
        f[16 + rows : 18 + rows] = below_ref[p, at].astype(F32) * keep
    for d in range(3):
        first = 15 - lead + d
        xs[d, p, c] = f[first : first + xs.shape[3]].astype(BF16)


def store_shifted(part, f2, hs, p, c, above, below):
    if part == "strips":
        f2[3:4] = f2[3:4] * above
        f2[28:29] = f2[28:29] * below
        for d in range(3):
            both = jnp.concatenate([f2[3 + d : 11 + d], f2[19 + d : 27 + d]], axis=0)
            hs[d, p, c] = both.astype(BF16)
        return
    nr = hs.shape[3]
    if part == "whole":
        f2[7:8] = f2[7:8] * above
        f2[8 + nr : 9 + nr] = f2[8 + nr : 9 + nr] * below
    for d in range(3):
        hs[d, p, c] = f2[7 + d : 7 + d + nr].astype(BF16)


def chunk_kernel(pick, part, packed, first, *refs):
    refs = list(refs)
    x_ref = refs.pop(0)
    halo = () if part == "inner" else (refs.pop(0), refs.pop(0))
    w1_ref, w2_ref, par_ref = refs[:3]
    refs = refs[3:]
    out_ref = refs.pop(0)
    trans_ref = None if packed else refs.pop(0)
    if first:
        x_hbm, w1_hbm, w2_hbm = x_ref, w1_ref, w2_ref
        x_ref, w1_ref, w2_ref = refs[:3]
        sem = refs.pop()
        copies = [
            pltpu.make_async_copy(x_hbm, x_ref, sem.at[0]),
            pltpu.make_async_copy(w1_hbm, w1_ref, sem.at[1]),
            pltpu.make_async_copy(w2_hbm, w2_ref, sem.at[2]),
        ]
        top_ref, bot_ref = refs[3:5]
        refs = refs[5:]
        for copy in copies:
            copy.start()
        for copy in copies:
            copy.wait()
        top_ref[...] = x_ref[:, :, 0:2]
        bot_ref[...] = x_ref[:, :, x_ref.shape[2] - 2 :]
    f_ref, xs, f2_ref, hs, fs = refs
    planes, cols, rows, ch = x_ref.shape
    nc, nr = fs.shape[1:3]
    ext = xs.shape[3]
    slots = f_ref.shape[0]
    c0 = pick() * nc
    for i in range(planes * (nc + 4)):
        p, c = divmod(i, nc + 4)
        at = c0 - 2 + c
        inside = jnp.logical_and(at >= 0, at < cols)
        at = jnp.clip(at, 0, cols - 1)
        keep = jnp.where(inside, 1.0, 0.0)
        load_shifted(part, x_ref, p, at, keep, f_ref.at[i % slots], xs, c, halo)
    here = lax.axis_index("rows")
    above = jnp.where(here == 0, 0.0, 1.0)
    below = jnp.where(here == lax.axis_size("rows") - 1, 0.0, 1.0)
    bias_one = par_ref[0:1]
    bias_two = par_ref[1:2]
    opacity = par_ref[2:3]
    weights = pair_weights(w1_ref)
    for p in range(planes):
        taps = []
        for j in range(4):
            for d in range(3):
                taps.append(jnp.concatenate([xs[d, p, g + j] for g in range(0, nc + 2, 2)], axis=0))
        y = jnp.dot(jnp.concatenate(taps, axis=1), weights, preferred_element_type=F32)
        for c in range(nc + 2):
            g, o = divmod(c, 2)
            v = gelu(y[g * ext : (g + 1) * ext, o * ch : (o + 1) * ch] + bias_one)
            if c == 0:
                v = v * jnp.where(c0 > 0, 1.0, 0.0)
            if c == nc + 1:
                v = v * jnp.where(c0 + nc < cols, 1.0, 0.0)
            f2 = f2_ref.at[p, c]
            f2[...] = v
            store_shifted(part, f2, hs, p, c, above, below)
    lane = lax.broadcasted_iota(jnp.int32, (nr, ch), 1)
    weights = pair_weights(w2_ref)
    logits = [jnp.zeros((nr, ch), F32) for _ in range(planes)]
    taps = []
    for j in range(4):
        for d in range(3):
            taps.append(
                jnp.concatenate(
                    [hs[d, p, g + j] for g in range(0, nc, 2) for p in range(planes)], axis=0
                )
            )
    y = jnp.dot(jnp.concatenate(taps, axis=1), weights, preferred_element_type=F32)
    for c in range(nc):
        g, o = divmod(c, 2)
        for p in range(planes):
            r0 = (g * planes + p) * nr
            f = gelu(y[r0 : r0 + nr, o * ch : (o + 1) * ch] + bias_two)
            total = jnp.sum(f * opacity, axis=1, keepdims=True)
            logits[p] = jnp.where(lane == c, total, logits[p])
            fs[p, c] = f
    parts = []
    trans = None
    for p in range(planes):
        alpha = 1.0 / (1.0 + jnp.exp(-(logits[p] + par_ref[3 + p : 4 + p])))
        if p == 0:
            parts.append(alpha)
            trans = 1.0 - alpha
        else:
            parts.append(trans * alpha)
            trans = trans * (1.0 - alpha)
    for c in range(nc):
        color = sum(parts[p][:, c : c + 1] * fs[p, c] for p in range(planes))
        out_ref[c] = color.astype(out_ref.dtype)
    if packed:
        high = trans.astype(BF16).astype(F32)
        low = pltpu.roll(trans - high, nc, axis=1)
        out_ref[nc] = jnp.where(lane < nc, high, low).astype(out_ref.dtype)
    else:
        trans_ref[...] = trans


def chunk(pick, nc, part, packed, first, x, halo, w1, w2, par):
    planes, cols, rows, ch = x.shape
    ext, nr = {"whole": (rows + 16, rows), "inner": (rows, rows - 16), "strips": (32, 16)}[part]
    if packed:
        out_shape = [jax.ShapeDtypeStruct((nc + 1, nr, ch), BF16)]
    else:
        out_shape = [
            jax.ShapeDtypeStruct((nc, nr, ch), F32),
            jax.ShapeDtypeStruct((nr, ch), F32),
        ]
    scratch = [
        pltpu.VMEM((8, rows + 32, ch), F32),
        pltpu.VMEM((3, planes, nc + 4, ext, ch), BF16),
        pltpu.VMEM((planes, nc + 2, ext, ch), F32),
        pltpu.VMEM((3, planes, nc + 2, nr, ch), BF16),
        pltpu.VMEM((planes, nc, nr, ch), F32),
    ]
    if part == "inner":
        halo = ()
    big = HBM if first else VM
    if first:
        edge = jax.ShapeDtypeStruct((planes, cols, 2, ch), x.dtype)
        out_shape += [jax.ShapeDtypeStruct(a.shape, a.dtype) for a in (x, w1, w2)] + [edge] * 2
        x, w1, w2 = (pltpu.with_memory_space_constraint(a, pltpu.HBM) for a in (x, w1, w2))
        scratch.append(pltpu.SemaphoreType.DMA((3,)))
    return pl.pallas_call(
        functools.partial(chunk_kernel, pick, part, packed, first),
        out_shape=out_shape,
        in_specs=[big] + [VM] * len(halo) + [big, big, VM],
        out_specs=[VM] * len(out_shape),
        scratch_shapes=scratch,
        compiler_params=pltpu.CompilerParams(vmem_limit_bytes=16 << 20),
        cost_estimate=pl.CostEstimate(flops=5 * 10**9, transcendentals=0, bytes_accessed=10**6),
    )(x, *halo, w1, w2, par)


def combine_kernel(splits, own_ref, trans_ref, *refs):
    refs = list(refs)
    out_ref = refs.pop()
    nc, rows, ch = own_ref.shape
    slabs = lax.axis_size("depth")
    here = lax.axis_index("depth")
    order = [here] + [lax.rem(here + slabs - s, slabs) for s in range(1, slabs)]
    groups = []
    for split in splits:
        groups.append([refs.pop(0) for _ in range(2 if split else 1)])
    for r0, nr in ((0, 8), (8, rows - 16), (rows - 8, 8)):
        views = []
        for group in groups:
            if len(group) == 1:
                views.append((group[0], r0))
            elif nr == 8:
                views.append((group[1], 0 if r0 == 0 else 8))
            else:
                views.append((group[0], 0))
        trans = [trans_ref[r0 : r0 + nr]]
        for ref, v0 in views:
            t = ref[nc, v0 : v0 + nr].astype(F32)
            trans.append(t + pltpu.roll(t, ch - nc, axis=1))
        scale = []
        for k in range(slabs):
            w = None
            for m in range(slabs):
                if m != k:
                    term = jnp.where(order[m] < order[k], trans[m], 1.0)
                    w = term if w is None else w * term
            scale.append(w)
        for c in range(nc):
            total = scale[0][:, c : c + 1] * own_ref[c, r0 : r0 + nr]
            for k, (ref, v0) in enumerate(views):
                total = total + scale[k + 1][:, c : c + 1] * ref[c, v0 : v0 + nr].astype(F32)
            out_ref[c, r0 : r0 + nr] = total


def combine(own, trans, got):
    flat = [a for group in got for a in group]
    return pl.pallas_call(
        functools.partial(combine_kernel, [len(group) == 2 for group in got]),
        out_shape=jax.ShapeDtypeStruct(own.shape, F32),
        in_specs=[VM] * (2 + len(flat)),
        out_specs=VM,
        compiler_params=pltpu.CompilerParams(vmem_limit_bytes=8 << 20),
    )(own, trans, *flat)


def send_on(value, step):
    slabs = lax.axis_size("depth")
    return lax.ppermute(value, "depth", [(i, (i + step) % slabs) for i in range(slabs)])


def exchange(value, axis, mask):
    pairs = [(i, i ^ mask) for i in range(lax.axis_size(axis))]
    return lax.ppermute(value, axis, pairs)


def pick_half(array, remaining, bit_set):
    shaped = array.reshape((remaining // 2, 2, -1) + array.shape[1:])
    first_half = shaped[:, 0].reshape((-1,) + array.shape[1:])
    second_half = shaped[:, 1].reshape((-1,) + array.shape[1:])
    keep = jnp.where(bit_set, second_half, first_half)
    other = jnp.where(bit_set, first_half, second_half)
    return (keep, other)


def butterfly(color, trans):
    position = lax.axis_index("depth")
    slabs = lax.axis_size("depth")
    for level in range(slabs.bit_length() - 1):
        remaining = slabs >> level
        bit_set = jnp.right_shift(position, level) % 2 == 1
        keep_color, send_color = pick_half(color, remaining, bit_set)
        keep_trans, send_trans = pick_half(trans, remaining, bit_set)
        got_color = exchange(send_color, "depth", 2**level)
        got_trans = exchange(send_trans, "depth", 2**level)
        color = jnp.where(
            bit_set,
            got_color + got_trans[..., None] * keep_color,
            keep_color + keep_trans[..., None] * got_color,
        )
        trans = keep_trans * got_trans
    return color


def per_device(volume, conv_one, bias_one, conv_two, bias_two, opacity_weight, opacity_bias):
    planes, cols, rows, ch = volume.shape
    slabs = lax.axis_size("depth")
    size = lax.axis_size("rows")
    par = jnp.concatenate(
        [
            jnp.stack([bias_one, bias_two, opacity_weight]),
            jnp.broadcast_to(opacity_bias[:, None], (planes, ch)),
        ]
    )
    up = [(i, i + 1) for i in range(size - 1)]
    down = [(i + 1, i) for i in range(size - 1)]
    if slabs != 4:
        top, bot = edges(volume)
        halo = (lax.ppermute(bot, "rows", up), lax.ppermute(top, "rows", down))
        nc = 16
        args = (nc, "whole", False, False, volume, halo, conv_one, conv_two, par)
        done = [chunk(functools.partial(jnp.int32, i), *args) for i in range(cols // nc)]
        color = jnp.concatenate([c for c, _ in done])
        trans = jnp.concatenate([jnp.transpose(t[:, :nc]) for _, t in done])
        return butterfly(color, trans)
    nc = cols // slabs

    def to(step):
        return lambda: lax.rem(lax.axis_index("depth") + step, slabs)

    one, x, w1, w2, top, bot = chunk(
        to(1), nc, "inner", True, True, volume, (), conv_one, conv_two, par
    )
    got_one = send_on(one, 1)
    above = lax.ppermute(bot, "rows", up)
    below = lax.ppermute(top, "rows", down)
    (two,) = chunk(to(2), nc, "inner", True, False, x, (), w1, w2, par)
    got_two = send_on(two, 2)
    x, above, below, two, got_one = lax.optimization_barrier((x, above, below, two, got_one))
    halo = (above, below)
    (one_strips,) = chunk(to(1), nc, "strips", True, False, x, halo, w1, w2, par)
    got_one_strips = send_on(one_strips, 1)
    x, one_strips = lax.optimization_barrier((x, one_strips))
    (two_strips,) = chunk(to(2), nc, "strips", True, False, x, halo, w1, w2, par)
    got_two_strips = send_on(two_strips, 2)
    x, two_strips = lax.optimization_barrier((x, two_strips))
    (three,) = chunk(to(3), nc, "whole", True, False, x, halo, w1, w2, par)
    got_three = send_on(three, 3)
    x, three = lax.optimization_barrier((x, three))
    own, trans = chunk(to(0), nc, "whole", False, False, x, halo, w1, w2, par)
    return combine(own, trans, [(got_one, got_one_strips), (got_two, got_two_strips), (got_three,)])


def solution(mesh):
    in_specs = (P(("grp", "depth"), None, "rows", None), P(), P(), P(), P(), P(), P("depth"))
    out_specs = P(("grp", "depth"), "rows", None)
    return jax.shard_map(
        per_device, mesh=mesh, in_specs=in_specs, out_specs=out_specs, check_vma=False
    )
```

```python
import functools

import jax
import jax.numpy as jnp
from jax import lax
from jax.experimental import pallas as pl
from jax.experimental.pallas import tpu as pltpu
from jax.sharding import PartitionSpec as P

VM = pl.BlockSpec(memory_space=pltpu.VMEM)
HBM = pl.BlockSpec(memory_space=pltpu.HBM)
F32 = jnp.float32
BF16 = jnp.bfloat16

PIECE = ((3, 2, 1, 0), (2, 0, 3, 1), (1, 3, 0, 2), (0, 1, 2, 3))
FAR = [(0, 1), (3, 2)]
NEAR = [(1, 2), (2, 1)]
SECOND = [(0, 2), (3, 1), (1, 0), (2, 3)]
THIRD = [(0, 1), (3, 2), (1, 3), (2, 0)]
MERGE = (0, 1, 2, 0)
KEYS = ((0, 1, 2, 3), (9, 2, 1, 9), (1, 3, 0, 2), (2, 0, 3, 0))


def gelu(x):
    c = 0.7978845608028654
    half = 0.5 * x
    return half + half * jnp.tanh(x * (c + (c * 0.044715) * (x * x)))


def pair_weights(w_ref):
    zero = jnp.zeros((w_ref.shape[2], w_ref.shape[3]), w_ref.dtype)
    blocks = []
    for j in range(4):
        for d in range(3):
            first = w_ref[j, d] if j < 3 else zero
            second = w_ref[j - 1, d] if j > 0 else zero
            blocks.append(jnp.concatenate([first, second], axis=1))
    return jnp.concatenate(blocks, axis=0)


def odd_row():
    return lax.rem(lax.axis_index("rows"), 2) == 1


def edges_kernel(x_hbm, one_ref, two_ref, buf, sem):
    rows = x_hbm.shape[2]
    a = pltpu.make_async_copy(x_hbm.at[:, :, pl.ds(0, 8)], buf.at[0], sem.at[0])
    b = pltpu.make_async_copy(x_hbm.at[:, :, pl.ds(rows - 8, 8)], buf.at[1], sem.at[1])
    a.start()
    b.start()
    a.wait()
    b.wait()

    @pl.when(odd_row())
    def _():
        one_ref[...] = buf[0, :, :, 0:2]
        two_ref[...] = buf[1, :, :, 6:8]

    @pl.when(jnp.logical_not(odd_row()))
    def _():
        one_ref[...] = buf[1, :, :, 6:8]
        two_ref[...] = buf[0, :, :, 0:2]


def edges(x):
    planes, cols, rows, ch = x.shape
    shape = jax.ShapeDtypeStruct((planes, cols, 2, ch), x.dtype)
    return pl.pallas_call(
        edges_kernel,
        out_shape=(shape, shape),
        in_specs=[HBM],
        out_specs=(VM, VM),
        scratch_shapes=[
            pltpu.VMEM((2, planes, cols, 8, ch), x.dtype),
            pltpu.SemaphoreType.DMA((2,)),
        ],
        compiler_params=pltpu.CompilerParams(vmem_limit_bytes=8 << 20),
    )(pltpu.with_memory_space_constraint(x, pltpu.HBM))


def load_kernel(x_hbm, w1_hbm, w2_hbm, b1_hbm, b2_hbm, ow_hbm, ob_ref, x_ref, w1_ref, w2_ref, par_ref, sem):
    pieces = 4
    step = x_ref.shape[1] // pieces
    pairs = [
        (w1_hbm, w1_ref),
        (w2_hbm, w2_ref),
        (b1_hbm, par_ref.at[0]),
        (b2_hbm, par_ref.at[1]),
        (ow_hbm, par_ref.at[2]),
    ]
    for i in range(pieces):
        at = (slice(None), pl.ds(i * step, step))
        pairs.append((x_hbm.at[at], x_ref.at[at]))
    copies = [pltpu.make_async_copy(src, dst, sem.at[i]) for i, (src, dst) in enumerate(pairs)]
    for copy in copies:
        copy.start()
    for p in range(x_ref.shape[0]):
        par_ref[3 + p : 4 + p] = jnp.full((1, x_ref.shape[3]), ob_ref[p])
    for copy in copies:
        copy.wait()


def load(x, w1, w2, b1, b2, ow, ob):
    args = [pltpu.with_memory_space_constraint(a, pltpu.HBM) for a in (x, w1, w2, b1, b2, ow)]
    out_shape = [jax.ShapeDtypeStruct(a.shape, a.dtype) for a in (x, w1, w2)]
    out_shape.append(jax.ShapeDtypeStruct((3 + x.shape[0], x.shape[3]), F32))
    return pl.pallas_call(
        load_kernel,
        out_shape=out_shape,
        in_specs=[HBM] * 6 + [pl.BlockSpec(memory_space=pltpu.SMEM)],
        out_specs=[VM] * 4,
        scratch_shapes=[pltpu.SemaphoreType.DMA((9,))],
        compiler_params=pltpu.CompilerParams(vmem_limit_bytes=8 << 20),
        cost_estimate=pl.CostEstimate(flops=10**9, transcendentals=0, bytes_accessed=10**6),
    )(*args, ob)


def chunk_kernel(pick, packed, x_ref, one_ref, two_ref, w1_ref, w2_ref, par_ref, *refs):
    refs = list(refs)
    out_ref = refs.pop(0)
    trans_ref = None if packed else refs.pop(0)
    f_ref, xs, f2_ref, hs, fs = refs
    planes, cols, rows, ch = x_ref.shape
    nc, nr = fs.shape[1:3]
    ext = xs.shape[3]
    slots = f_ref.shape[0]
    c0 = pick() * nc
    odd = odd_row()
    for i in range(planes * (nc + 4)):
        p, c = divmod(i, nc + 4)
        at = c0 - 2 + c
        inside = jnp.logical_and(at >= 0, at < cols)
        at = jnp.clip(at, 0, cols - 1)
        keep = jnp.where(inside, 1.0, 0.0)
        f = f_ref.at[i % slots]
        one = one_ref[p, at].astype(F32)
        two = two_ref[p, at].astype(F32)
        f[16 : 16 + rows] = x_ref[p, at].astype(F32) * keep
        f[14:16] = jnp.where(odd, one, two) * keep
        f[16 + rows : 18 + rows] = jnp.where(odd, two, one) * keep
        for d in range(3):
            xs[d, p, c] = f[7 + d : 7 + d + ext].astype(BF16)
    here = lax.axis_index("rows")
    above = jnp.where(here == 0, 0.0, 1.0)
    below = jnp.where(here == lax.axis_size("rows") - 1, 0.0, 1.0)
    bias_one = par_ref[0:1]
    bias_two = par_ref[1:2]
    opacity = par_ref[2:3]
    weights = pair_weights(w1_ref)
    for p in range(planes):
        taps = []
        for j in range(4):
            for d in range(3):
                taps.append(jnp.concatenate([xs[d, p, g + j] for g in range(0, nc + 2, 2)], axis=0))
        y = jnp.dot(jnp.concatenate(taps, axis=1), weights, preferred_element_type=F32)
        for c in range(nc + 2):
            g, o = divmod(c, 2)
            v = gelu(y[g * ext : (g + 1) * ext, o * ch : (o + 1) * ch] + bias_one)
            if c == 0:
                v = v * jnp.where(c0 > 0, 1.0, 0.0)
            if c == nc + 1:
                v = v * jnp.where(c0 + nc < cols, 1.0, 0.0)
            f2 = f2_ref.at[p, c]
            f2[...] = v
            f2[7:8] = f2[7:8] * above
            f2[8 + rows : 9 + rows] = f2[8 + rows : 9 + rows] * below
            for d in range(3):
                hs[d, p, c] = f2[7 + d : 7 + d + rows].astype(BF16)
    lane = lax.broadcasted_iota(jnp.int32, (nr, ch), 1)
    weights = pair_weights(w2_ref)
    logits = [jnp.zeros((nr, ch), F32) for _ in range(planes)]
    taps = []
    for j in range(4):
        for d in range(3):
            taps.append(
                jnp.concatenate(
                    [hs[d, p, g + j] for g in range(0, nc, 2) for p in range(planes)], axis=0
                )
            )
    y = jnp.dot(jnp.concatenate(taps, axis=1), weights, preferred_element_type=F32)
    for c in range(nc):
        g, o = divmod(c, 2)
        for p in range(planes):
            r0 = (g * planes + p) * nr
            f = gelu(y[r0 : r0 + nr, o * ch : (o + 1) * ch] + bias_two)
            total = jnp.sum(f * opacity, axis=1, keepdims=True)
            logits[p] = jnp.where(lane == c, total, logits[p])
            fs[p, c] = f
    parts = []
    trans = None
    for p in range(planes):
        alpha = 1.0 / (1.0 + jnp.exp(-(logits[p] + par_ref[3 + p : 4 + p])))
        if p == 0:
            parts.append(alpha)
            trans = 1.0 - alpha
        else:
            parts.append(trans * alpha)
            trans = trans * (1.0 - alpha)
    for c in range(nc):
        color = sum(parts[p][:, c : c + 1] * fs[p, c] for p in range(planes))
        out_ref[c] = color.astype(out_ref.dtype)
    if packed:
        out_ref[nc] = pack_trans(trans, nc)
    else:
        trans_ref[...] = trans


def chunk(pick, nc, packed, x, one, two, w1, w2, par):
    planes, cols, rows, ch = x.shape
    ext = rows + 16
    if packed:
        out_shape = [jax.ShapeDtypeStruct((nc + 1, rows, ch), BF16)]
    else:
        out_shape = [
            jax.ShapeDtypeStruct((nc, rows, ch), F32),
            jax.ShapeDtypeStruct((rows, ch), F32),
        ]
    return pl.pallas_call(
        functools.partial(chunk_kernel, pick, packed),
        out_shape=out_shape,
        in_specs=[VM] * 6,
        out_specs=[VM] * len(out_shape),
        scratch_shapes=[
            pltpu.VMEM((8, rows + 32, ch), F32),
            pltpu.VMEM((3, planes, nc + 4, ext, ch), BF16),
            pltpu.VMEM((planes, nc + 2, ext, ch), F32),
            pltpu.VMEM((3, planes, nc + 2, rows, ch), BF16),
            pltpu.VMEM((planes, nc, rows, ch), F32),
        ],
        compiler_params=pltpu.CompilerParams(vmem_limit_bytes=16 << 20),
        cost_estimate=pl.CostEstimate(flops=5 * 10**9, transcendentals=0, bytes_accessed=10**6),
    )(x, one, two, w1, w2, par)


def lookup(table):
    here = lax.axis_index("depth")
    value = jnp.int32(table[-1])
    for i in range(len(table) - 1):
        value = jnp.where(here == i, table[i], value)
    return value


def unpack_trans(packed):
    nc = packed.shape[0] - 1
    t = packed[nc].astype(F32)
    return t + pltpu.roll(t, t.shape[1] - nc, axis=1)


def pack_trans(trans, nc):
    lane = lax.broadcasted_iota(jnp.int32, trans.shape, 1)
    high = trans.astype(BF16).astype(F32)
    low = pltpu.roll(trans - high, nc, axis=1)
    return jnp.where(lane < nc, high, low).astype(BF16)


def merge_kernel(own_ref, trans_ref, got_ref, out_ref):
    nc = own_ref.shape[0]
    mine = trans_ref[...]
    theirs = unpack_trans(got_ref)
    role = lookup(MERGE)
    scale_own = jnp.where(role == 1, theirs, 1.0)
    scale_got = jnp.where(role == 2, mine, jnp.where(role == 1, 1.0, 0.0))
    for c in range(nc):
        color = scale_own[:, c : c + 1] * own_ref[c]
        color = color + scale_got[:, c : c + 1] * got_ref[c].astype(F32)
        out_ref[c] = color.astype(BF16)
    out_ref[nc] = pack_trans(jnp.where(role == 0, mine, mine * theirs), nc)


def merge(own, trans, got):
    return pl.pallas_call(
        merge_kernel,
        out_shape=jax.ShapeDtypeStruct(got.shape, BF16),
        in_specs=[VM] * 3,
        out_specs=VM,
        compiler_params=pltpu.CompilerParams(vmem_limit_bytes=8 << 20),
        cost_estimate=pl.CostEstimate(flops=10**9, transcendentals=0, bytes_accessed=10**6),
    )(own, trans, got)


def combine_kernel(own_ref, trans_ref, *refs):
    *got_refs, out_ref = refs
    nc = own_ref.shape[0]
    keys = [lookup(table) for table in KEYS]
    trans = [trans_ref[...]] + [unpack_trans(ref) for ref in got_refs]
    scale = []
    for k in range(len(trans)):
        w = None
        for m in range(len(trans)):
            if m != k:
                term = jnp.where(keys[m] < keys[k], trans[m], 1.0)
                w = term if w is None else w * term
        scale.append(w)
    for c in range(nc):
        total = scale[0][:, c : c + 1] * own_ref[c]
        for k, ref in enumerate(got_refs):
            total = total + scale[k + 1][:, c : c + 1] * ref[c].astype(F32)
        out_ref[c] = total


def combine(own, trans, got):
    return pl.pallas_call(
        combine_kernel,
        out_shape=jax.ShapeDtypeStruct(own.shape, F32),
        in_specs=[VM] * (2 + len(got)),
        out_specs=VM,
        compiler_params=pltpu.CompilerParams(vmem_limit_bytes=8 << 20),
    )(own, trans, *got)


def exchange(value, axis, mask):
    pairs = [(i, i ^ mask) for i in range(lax.axis_size(axis))]
    return lax.ppermute(value, axis, pairs)


def pick_half(array, remaining, bit_set):
    shaped = array.reshape((remaining // 2, 2, -1) + array.shape[1:])
    first_half = shaped[:, 0].reshape((-1,) + array.shape[1:])
    second_half = shaped[:, 1].reshape((-1,) + array.shape[1:])
    keep = jnp.where(bit_set, second_half, first_half)
    other = jnp.where(bit_set, first_half, second_half)
    return (keep, other)


def butterfly(color, trans):
    position = lax.axis_index("depth")
    slabs = lax.axis_size("depth")
    for level in range(slabs.bit_length() - 1):
        remaining = slabs >> level
        bit_set = jnp.right_shift(position, level) % 2 == 1
        keep_color, send_color = pick_half(color, remaining, bit_set)
        keep_trans, send_trans = pick_half(trans, remaining, bit_set)
        got_color = exchange(send_color, "depth", 2**level)
        got_trans = exchange(send_trans, "depth", 2**level)
        color = jnp.where(
            bit_set,
            got_color + got_trans[..., None] * keep_color,
            keep_color + keep_trans[..., None] * got_color,
        )
        trans = keep_trans * got_trans
    return color


def per_device(volume, conv_one, bias_one, conv_two, bias_two, opacity_weight, opacity_bias):
    planes, cols, rows, ch = volume.shape
    slabs = lax.axis_size("depth")
    size = lax.axis_size("rows")
    one, two = edges(volume)
    one = lax.ppermute(one, "rows", [(i, i ^ 1) for i in range(size)])
    inner = [(i, i + 1) for i in range(1, size - 1, 2)]
    two = lax.ppermute(two, "rows", inner + [(j, i) for i, j in inner])
    x, w1, w2, par = load(
        volume, conv_one, conv_two, bias_one, bias_two, opacity_weight, opacity_bias
    )
    args = (x, one, two, w1, w2, par)
    if slabs != 4:
        nc = 16
        done = [chunk(functools.partial(jnp.int32, i), nc, False, *args) for i in range(cols // nc)]
        color = jnp.concatenate([c for c, _ in done])
        trans = jnp.concatenate([jnp.transpose(t[:, :nc]) for _, t in done])
        return butterfly(color, trans)
    nc = cols // slabs

    def piece(slot, packed):
        pick = functools.partial(lookup, [order[slot] for order in PIECE])
        return chunk(pick, nc, packed, x, one, two, w1, w2, par)

    (first,) = piece(0, True)
    far = lax.ppermute(first, "depth", FAR)
    near = lax.ppermute(first, "depth", NEAR)
    (second,) = piece(1, True)
    second = lax.ppermute(second, "depth", SECOND)
    third = lax.ppermute(merge(*piece(2, False), far), "depth", THIRD)
    own, trans = piece(3, False)
    return combine(own, trans, [near, second, third])


def solution(mesh):
    in_specs = (P(("grp", "depth"), None, "rows", None), P(), P(), P(), P(), P(), P("depth"))
    out_specs = P(("grp", "depth"), "rows", None)
    return jax.shard_map(
        per_device, mesh=mesh, in_specs=in_specs, out_specs=out_specs, check_vma=False
    )
```

```python
import functools

import jax
import jax.numpy as jnp
from jax import lax
from jax.experimental import pallas as pl
from jax.experimental.pallas import tpu as pltpu
from jax.sharding import PartitionSpec as P

VM = pl.BlockSpec(memory_space=pltpu.VMEM)
HBM = pl.BlockSpec(memory_space=pltpu.HBM)
F32 = jnp.float32
BF16 = jnp.bfloat16

PIECE = ((3, 2, 1, 0), (2, 0, 3, 1), (1, 3, 0, 2), (0, 1, 2, 3))
FAR = [(0, 1), (3, 2)]
NEAR = [(1, 2), (2, 1)]
SECOND = [(0, 2), (3, 1), (1, 0), (2, 3)]
THIRD = [(0, 1), (3, 2), (1, 3), (2, 0)]
MERGE = (0, 1, 2, 0)
KEYS = ((0, 1, 2, 3), (9, 2, 1, 9), (1, 3, 0, 2))
LAST_IN_FRONT = (0, 1, 0, 1)


def gelu(x):
    c = 0.7978845608028654
    half = 0.5 * x
    return half + half * jnp.tanh(x * (c + (c * 0.044715) * (x * x)))


def pair_weights(w_ref):
    zero = jnp.zeros((w_ref.shape[2], w_ref.shape[3]), w_ref.dtype)
    blocks = []
    for j in range(4):
        for d in range(3):
            first = w_ref[j, d] if j < 3 else zero
            second = w_ref[j - 1, d] if j > 0 else zero
            blocks.append(jnp.concatenate([first, second], axis=1))
    return jnp.concatenate(blocks, axis=0)


def odd_row():
    return lax.rem(lax.axis_index("rows"), 2) == 1


def edges_kernel(x_hbm, one_ref, two_ref, buf, sem):
    rows = x_hbm.shape[2]
    a = pltpu.make_async_copy(x_hbm.at[:, :, pl.ds(0, 8)], buf.at[0], sem.at[0])
    b = pltpu.make_async_copy(x_hbm.at[:, :, pl.ds(rows - 8, 8)], buf.at[1], sem.at[1])
    a.start()
    b.start()
    a.wait()
    b.wait()

    @pl.when(odd_row())
    def _():
        one_ref[...] = buf[0, :, :, 0:2]
        two_ref[...] = buf[1, :, :, 6:8]

    @pl.when(jnp.logical_not(odd_row()))
    def _():
        one_ref[...] = buf[1, :, :, 6:8]
        two_ref[...] = buf[0, :, :, 0:2]


def edges(x):
    planes, cols, rows, ch = x.shape
    shape = jax.ShapeDtypeStruct((planes, cols, 2, ch), x.dtype)
    return pl.pallas_call(
        edges_kernel,
        out_shape=(shape, shape),
        in_specs=[HBM],
        out_specs=(VM, VM),
        scratch_shapes=[
            pltpu.VMEM((2, planes, cols, 8, ch), x.dtype),
            pltpu.SemaphoreType.DMA((2,)),
        ],
        compiler_params=pltpu.CompilerParams(vmem_limit_bytes=8 << 20),
    )(pltpu.with_memory_space_constraint(x, pltpu.HBM))


def first_conv(xs, w1_ref, bias, c0, cols, emit):
    planes, wide, ext, ch = xs.shape[1:]
    count = wide - 2
    weights = pair_weights(w1_ref)
    for p in range(planes):
        taps = []
        for j in range(4):
            for d in range(3):
                taps.append(jnp.concatenate([xs[d, p, g + j] for g in range(0, count, 2)], axis=0))
        y = jnp.dot(jnp.concatenate(taps, axis=1), weights, preferred_element_type=F32)
        for c in range(count):
            g, o = divmod(c, 2)
            v = gelu(y[g * ext : (g + 1) * ext, o * ch : (o + 1) * ch] + bias)
            if c == 0:
                v = v * jnp.where(c0 > 0, 1.0, 0.0)
            if c == count - 1:
                v = v * jnp.where(c0 + count - 2 < cols, 1.0, 0.0)
            emit(p, c, v)


def row_masks():
    here = lax.axis_index("rows")
    above = jnp.where(here == 0, 0.0, 1.0)
    below = jnp.where(here == lax.axis_size("rows") - 1, 0.0, 1.0)
    return above, below


def column(c0, c, cols):
    at = c0 - 2 + c
    inside = jnp.logical_and(at >= 0, at < cols)
    return jnp.clip(at, 0, cols - 1), jnp.where(inside, 1.0, 0.0)


def halo_rows(one_ref, two_ref, p, at, odd):
    one = one_ref[p, at].astype(F32)
    two = two_ref[p, at].astype(F32)
    return jnp.where(odd, one, two), jnp.where(odd, two, one)


def second_half(hs, fs, w2_ref, par_ref, out_ref, trans_ref):
    planes, nc, rows, ch = fs.shape
    bias = par_ref[1:2]
    opacity = par_ref[2:3]
    lane = lax.broadcasted_iota(jnp.int32, (rows, ch), 1)
    logits = [jnp.zeros((rows, ch), F32) for _ in range(planes)]
    taps = []
    for j in range(4):
        for d in range(3):
            taps.append(
                jnp.concatenate(
                    [hs[d, p, g + j] for g in range(0, nc, 2) for p in range(planes)], axis=0
                )
            )
    y = jnp.dot(jnp.concatenate(taps, axis=1), pair_weights(w2_ref), preferred_element_type=F32)
    for c in range(nc):
        g, o = divmod(c, 2)
        for p in range(planes):
            r0 = (g * planes + p) * rows
            f = gelu(y[r0 : r0 + rows, o * ch : (o + 1) * ch] + bias)
            total = jnp.sum(f * opacity, axis=1, keepdims=True)
            logits[p] = jnp.where(lane == c, total, logits[p])
            fs[p, c] = f
    parts = []
    trans = None
    for p in range(planes):
        alpha = 1.0 / (1.0 + jnp.exp(-(logits[p] + par_ref[3 + p : 4 + p])))
        if p == 0:
            parts.append(alpha)
            trans = 1.0 - alpha
        else:
            parts.append(trans * alpha)
            trans = trans * (1.0 - alpha)
    for c in range(nc):
        color = sum(parts[p][:, c : c + 1] * fs[p, c] for p in range(planes))
        if trans_ref is None:
            out_ref[c * rows : (c + 1) * rows] = color.astype(BF16)
        else:
            out_ref[c] = color
    if trans_ref is None:
        out_ref[nc * rows :] = pack_trans(trans, nc)
    else:
        trans_ref[...] = trans


def outputs(nc, rows, ch, packed):
    if packed:
        return [jax.ShapeDtypeStruct((nc * rows + rows // folds(nc, rows, ch), ch), BF16)]
    return [jax.ShapeDtypeStruct((nc, rows, ch), F32), jax.ShapeDtypeStruct((rows, ch), F32)]


def call(kernel, args, in_specs, out_shape, scratch):
    return pl.pallas_call(
        kernel,
        out_shape=out_shape,
        in_specs=in_specs,
        out_specs=[VM] * len(out_shape),
        scratch_shapes=scratch,
        compiler_params=pltpu.CompilerParams(vmem_limit_bytes=16 << 20),
        cost_estimate=pl.CostEstimate(flops=5 * 10**9, transcendentals=0, bytes_accessed=10**6),
    )(*args)


def chunk_kernel(pick, packed, x_ref, one_ref, two_ref, w1_ref, w2_ref, par_ref, *refs):
    refs = list(refs)
    out_ref = refs.pop(0)
    trans_ref = None if packed else refs.pop(0)
    f_ref, xs, f2_ref, hs, fs = refs
    planes, cols, rows, ch = x_ref.shape
    nc = fs.shape[1]
    ext = xs.shape[3]
    c0 = pick() * nc
    odd = odd_row()
    for i in range(planes * (nc + 4)):
        p, c = divmod(i, nc + 4)
        at, keep = column(c0, c, cols)
        f = f_ref.at[i % f_ref.shape[0]]
        upper, lower = halo_rows(one_ref, two_ref, p, at, odd)
        f[16 : 16 + rows] = x_ref[p, at].astype(F32) * keep
        f[14:16] = upper * keep
        f[16 + rows : 18 + rows] = lower * keep
        for d in range(3):
            xs[d, p, c] = f[7 + d : 7 + d + ext].astype(BF16)
    above, below = row_masks()

    def emit(p, c, v):
        f2 = f2_ref.at[p, c]
        f2[...] = v
        f2[7:8] = f2[7:8] * above
        f2[8 + rows : 9 + rows] = f2[8 + rows : 9 + rows] * below
        for d in range(3):
            hs[d, p, c] = f2[7 + d : 7 + d + rows].astype(BF16)

    first_conv(xs, w1_ref, par_ref[0:1], c0, cols, emit)
    second_half(hs, fs, w2_ref, par_ref, out_ref, trans_ref)


def chunk(pick, nc, packed, x, one, two, w1, w2, par):
    planes, cols, rows, ch = x.shape
    ext = rows + 16
    scratch = [
        pltpu.VMEM((8, rows + 32, ch), F32),
        pltpu.VMEM((3, planes, nc + 4, ext, ch), BF16),
        pltpu.VMEM((planes, nc + 2, ext, ch), F32),
        pltpu.VMEM((3, planes, nc + 2, rows, ch), BF16),
        pltpu.VMEM((planes, nc, rows, ch), F32),
    ]
    kernel = functools.partial(chunk_kernel, pick, packed)
    args = (x, one, two, w1, w2, par)
    return call(kernel, args, [VM] * 6, outputs(nc, rows, ch, packed), scratch)


def head_kernel(pick, nc, x_ref, w1_hbm, w2_hbm, b1_hbm, b2_hbm, ow_hbm, ob_ref, *refs):
    hid_ref, w1_ref, w2_ref, par_ref, f_ref, xs, sem = refs
    planes, cols, rows, ch = x_ref.shape
    pairs = [
        (w1_hbm, w1_ref),
        (b1_hbm, par_ref.at[0]),
        (w2_hbm, w2_ref),
        (b2_hbm, par_ref.at[1]),
        (ow_hbm, par_ref.at[2]),
    ]
    copies = [pltpu.make_async_copy(src, dst, sem.at[i]) for i, (src, dst) in enumerate(pairs)]
    for copy in copies:
        copy.start()
    for p in range(planes):
        par_ref[3 + p : 4 + p] = jnp.full((1, ch), ob_ref[p])
    c0 = pick() * nc
    for i in range(planes * (nc + 4)):
        p, c = divmod(i, nc + 4)
        at, keep = column(c0, c, cols)
        f = f_ref.at[i % f_ref.shape[0]]
        f[16 : 16 + rows] = x_ref[p, at].astype(F32) * keep
        for d in range(3):
            xs[d, p, c] = f[15 + d : 15 + d + rows].astype(BF16)
    copies[0].wait()
    copies[1].wait()

    def emit(p, c, v):
        hid_ref[p, c, 8 : 8 + rows] = v

    first_conv(xs, w1_ref, par_ref[0:1], c0, cols, emit)
    for copy in copies[2:]:
        copy.wait()


def head(pick, nc, x, w1, w2, b1, b2, ow, ob):
    planes, cols, rows, ch = x.shape
    args = [pltpu.with_memory_space_constraint(a, pltpu.HBM) for a in (w1, w2, b1, b2, ow)]
    out_shape = [
        jax.ShapeDtypeStruct((planes, nc + 2, rows + 16, ch), F32),
        jax.ShapeDtypeStruct(w1.shape, w1.dtype),
        jax.ShapeDtypeStruct(w2.shape, w2.dtype),
        jax.ShapeDtypeStruct((3 + planes, ch), F32),
    ]
    scratch = [
        pltpu.VMEM((8, rows + 32, ch), F32),
        pltpu.VMEM((3, planes, nc + 4, rows, ch), BF16),
        pltpu.SemaphoreType.DMA((5,)),
    ]
    in_specs = [VM] + [HBM] * 5 + [pl.BlockSpec(memory_space=pltpu.SMEM)]
    kernel = functools.partial(head_kernel, pick, nc)
    return call(kernel, (x, *args, ob), in_specs, out_shape, scratch)


def tail_kernel(pick, x_ref, one_ref, two_ref, hid_ref, w1_ref, w2_ref, par_ref, out_ref, *refs):
    f_ref, xs, edge_ref, f2_ref, hs, fs = refs
    planes, cols, rows, ch = x_ref.shape
    nc = fs.shape[1]
    c0 = pick() * nc
    odd = odd_row()
    for i in range(planes * (nc + 4)):
        p, c = divmod(i, nc + 4)
        at, keep = column(c0, c, cols)
        f = f_ref.at[i % f_ref.shape[0]]
        upper, lower = halo_rows(one_ref, two_ref, p, at, odd)
        f[6:8] = upper * keep
        f[8:16] = x_ref[p, at, 0:8].astype(F32) * keep
        f[24:32] = x_ref[p, at, rows - 8 : rows].astype(F32) * keep
        f[32:34] = lower * keep
        for d in range(3):
            both = jnp.concatenate([f[3 + d : 11 + d], f[27 + d : 35 + d]], axis=0)
            xs[d, p, c] = both.astype(BF16)
    above, below = row_masks()

    def emit(p, c, v):
        edge = edge_ref.at[p, c]
        edge[...] = v
        f2 = f2_ref.at[p, c]
        f2[8 : 8 + rows] = hid_ref[p, c, 8 : 8 + rows]
        f2[7:8] = edge[3:4] * above
        f2[8:9] = edge[4:5]
        f2[7 + rows : 8 + rows] = edge[11:12]
        f2[8 + rows : 9 + rows] = edge[12:13] * below
        for d in range(3):
            hs[d, p, c] = f2[7 + d : 7 + d + rows].astype(BF16)

    first_conv(xs, w1_ref, par_ref[0:1], c0, cols, emit)
    second_half(hs, fs, w2_ref, par_ref, out_ref, None)


def tail(pick, nc, x, one, two, hid, w1, w2, par):
    planes, cols, rows, ch = x.shape
    scratch = [
        pltpu.VMEM((8, 40, ch), F32),
        pltpu.VMEM((3, planes, nc + 4, 16, ch), BF16),
        pltpu.VMEM((planes, nc + 2, 16, ch), F32),
        pltpu.VMEM((planes, nc + 2, rows + 16, ch), F32),
        pltpu.VMEM((3, planes, nc + 2, rows, ch), BF16),
        pltpu.VMEM((planes, nc, rows, ch), F32),
    ]
    args = (x, one, two, hid, w1, w2, par)
    kernel = functools.partial(tail_kernel, pick)
    return call(kernel, args, [VM] * 7, outputs(nc, rows, ch, True), scratch)[0]


def lookup(table):
    here = lax.axis_index("depth")
    value = jnp.int32(table[-1])
    for i in range(len(table) - 1):
        value = jnp.where(here == i, table[i], value)
    return value


def folds(nc, rows, ch):
    return min(rows // 16, ch // (2 * nc))


def unpack_trans(ref, nc, rows):
    ch = ref.shape[1]
    fold = folds(nc, rows, ch)
    block = ref[nc * rows :].astype(F32)
    block = block + pltpu.roll(block, ch - nc, axis=1)
    parts = [block] + [pltpu.roll(block, ch - 2 * nc * q, axis=1) for q in range(1, fold)]
    return jnp.concatenate(parts, axis=0)


def pack_trans(trans, nc):
    rows, ch = trans.shape
    fold = folds(nc, rows, ch)
    size = rows // fold
    lane = lax.broadcasted_iota(jnp.int32, trans.shape, 1)
    high = trans.astype(BF16).astype(F32)
    low = pltpu.roll(trans - high, nc, axis=1)
    both = jnp.where(lane < nc, high, jnp.where(lane < 2 * nc, low, 0.0))
    block = both[:size]
    for q in range(1, fold):
        block = block + pltpu.roll(both[q * size : (q + 1) * size], 2 * nc * q, axis=1)
    return block.astype(BF16)


def merge_kernel(own_ref, trans_ref, got_ref, out_ref):
    nc = own_ref.shape[0]
    mine = trans_ref[...]
    rows = own_ref.shape[1]
    theirs = unpack_trans(got_ref, nc, rows)
    role = lookup(MERGE)
    scale_own = jnp.where(role == 1, theirs, 1.0)
    scale_got = jnp.where(role == 2, mine, jnp.where(role == 1, 1.0, 0.0))
    for c in range(nc):
        color = scale_own[:, c : c + 1] * own_ref[c]
        at = slice(c * rows, (c + 1) * rows)
        color = color + scale_got[:, c : c + 1] * got_ref[at].astype(F32)
        out_ref[at] = color.astype(BF16)
    out_ref[nc * rows :] = pack_trans(jnp.where(role == 0, mine, mine * theirs), nc)


def merge(own, trans, got):
    return pl.pallas_call(
        merge_kernel,
        out_shape=jax.ShapeDtypeStruct(got.shape, BF16),
        in_specs=[VM] * 3,
        out_specs=VM,
        compiler_params=pltpu.CompilerParams(vmem_limit_bytes=8 << 20),
        cost_estimate=pl.CostEstimate(flops=10**9, transcendentals=0, bytes_accessed=10**6),
    )(own, trans, got)


def gather_kernel(own_ref, trans_ref, *refs):
    *got_refs, out_ref, out_trans_ref = refs
    nc, rows = own_ref.shape[:2]
    keys = [lookup(table) for table in KEYS]
    trans = [trans_ref[...]] + [unpack_trans(ref, nc, rows) for ref in got_refs]
    scale = []
    through = None
    for k in range(len(trans)):
        w = None
        for m in range(len(trans)):
            if m != k:
                term = jnp.where(keys[m] < keys[k], trans[m], 1.0)
                w = term if w is None else w * term
        scale.append(w)
        term = jnp.where(keys[k] == 9, 1.0, trans[k])
        through = term if through is None else through * term
    for c in range(nc):
        total = scale[0][:, c : c + 1] * own_ref[c]
        for k, ref in enumerate(got_refs):
            at = slice(c * rows, (c + 1) * rows)
            total = total + scale[k + 1][:, c : c + 1] * ref[at].astype(F32)
        out_ref[c] = total
    out_trans_ref[...] = through


def finish_kernel(near_ref, trans_ref, got_ref, out_hbm, out, sem):
    nc, rows = near_ref.shape[:2]
    front = lookup(LAST_IN_FRONT) == 1
    theirs = unpack_trans(got_ref, nc, rows)
    scale_near = jnp.where(front, theirs, 1.0)
    scale_got = jnp.where(front, 1.0, trans_ref[...])
    pieces = sem.shape[0]
    step = nc // pieces
    copies = []
    for i in range(pieces):
        for c in range(i * step, (i + 1) * step):
            got = got_ref[c * rows : (c + 1) * rows].astype(F32)
            out[c] = scale_near[:, c : c + 1] * near_ref[c] + scale_got[:, c : c + 1] * got
        at = pl.ds(i * step, step)
        copies.append(pltpu.make_async_copy(out.at[at], out_hbm.at[at], sem.at[i]))
        copies[-1].start()
    for copy in copies:
        copy.wait()


def combine(own, trans, got):
    color = jax.ShapeDtypeStruct(own.shape, F32)
    near, trans = pl.pallas_call(
        gather_kernel,
        out_shape=[color, jax.ShapeDtypeStruct(trans.shape, F32)],
        in_specs=[VM] * 4,
        out_specs=[VM] * 2,
        compiler_params=pltpu.CompilerParams(vmem_limit_bytes=8 << 20),
        cost_estimate=pl.CostEstimate(flops=10**9, transcendentals=0, bytes_accessed=10**6),
    )(own, trans, *got[:2])
    return pl.pallas_call(
        finish_kernel,
        out_shape=color,
        in_specs=[VM] * 3,
        out_specs=HBM,
        scratch_shapes=[pltpu.VMEM(own.shape, F32), pltpu.SemaphoreType.DMA((4,))],
        compiler_params=pltpu.CompilerParams(vmem_limit_bytes=8 << 20),
    )(near, trans, got[2])


def exchange(value, axis, mask):
    pairs = [(i, i ^ mask) for i in range(lax.axis_size(axis))]
    return lax.ppermute(value, axis, pairs)


def pick_half(array, remaining, bit_set):
    shaped = array.reshape((remaining // 2, 2, -1) + array.shape[1:])
    first_half = shaped[:, 0].reshape((-1,) + array.shape[1:])
    second_half = shaped[:, 1].reshape((-1,) + array.shape[1:])
    keep = jnp.where(bit_set, second_half, first_half)
    other = jnp.where(bit_set, first_half, second_half)
    return (keep, other)


def butterfly(color, trans):
    position = lax.axis_index("depth")
    slabs = lax.axis_size("depth")
    for level in range(slabs.bit_length() - 1):
        remaining = slabs >> level
        bit_set = jnp.right_shift(position, level) % 2 == 1
        keep_color, send_color = pick_half(color, remaining, bit_set)
        keep_trans, send_trans = pick_half(trans, remaining, bit_set)
        got_color = exchange(send_color, "depth", 2**level)
        got_trans = exchange(send_trans, "depth", 2**level)
        color = jnp.where(
            bit_set,
            got_color + got_trans[..., None] * keep_color,
            keep_color + keep_trans[..., None] * got_color,
        )
        trans = keep_trans * got_trans
    return color


def per_device(volume, conv_one, bias_one, conv_two, bias_two, opacity_weight, opacity_bias):
    planes, cols, rows, ch = volume.shape
    slabs = lax.axis_size("depth")
    size = lax.axis_size("rows")
    one, two = edges(volume)
    one = lax.ppermute(one, "rows", [(i, i ^ 1) for i in range(size)])
    inner = [(i, i + 1) for i in range(1, size - 1, 2)]
    two = lax.ppermute(two, "rows", inner + [(j, i) for i, j in inner])
    if slabs != 4:
        par = jnp.concatenate(
            [
                jnp.stack([bias_one, bias_two, opacity_weight]),
                jnp.broadcast_to(opacity_bias[:, None], (planes, ch)),
            ]
        )
        args = (16, False, volume, one, two, conv_one, conv_two, par)
        done = [chunk(functools.partial(jnp.int32, i), *args) for i in range(cols // 16)]
        color = jnp.concatenate([c for c, _ in done])
        trans = jnp.concatenate([jnp.transpose(t[:, :16]) for _, t in done])
        return butterfly(color, trans)
    nc = cols // slabs
    picks = [functools.partial(lookup, [order[slot] for order in PIECE]) for slot in range(4)]
    hid, w1, w2, par = head(
        picks[0], nc, volume, conv_one, conv_two, bias_one, bias_two, opacity_weight, opacity_bias
    )

    def piece(slot, packed):
        return chunk(picks[slot], nc, packed, volume, one, two, w1, w2, par)

    first = tail(picks[0], nc, volume, one, two, hid, w1, w2, par)
    far = lax.ppermute(first, "depth", FAR)
    near = lax.ppermute(first, "depth", NEAR)
    (second,) = piece(1, True)
    second = lax.ppermute(second, "depth", SECOND)
    third = lax.ppermute(merge(*piece(2, False), far), "depth", THIRD)
    own, trans = piece(3, False)
    return combine(own, trans, [near, second, third])


def solution(mesh):
    in_specs = (P(("grp", "depth"), None, "rows", None), P(), P(), P(), P(), P(), P("depth"))
    out_specs = P(("grp", "depth"), "rows", None)
    return jax.shard_map(
        per_device, mesh=mesh, in_specs=in_specs, out_specs=out_specs, check_vma=False
    )
```

```python
import functools

import jax
import jax.numpy as jnp
from jax import lax
from jax.experimental import pallas as pl
from jax.experimental.pallas import tpu as pltpu
from jax.sharding import PartitionSpec as P

VM = pl.BlockSpec(memory_space=pltpu.VMEM)
HBM = pl.BlockSpec(memory_space=pltpu.HBM)
F32 = jnp.float32
BF16 = jnp.bfloat16

PIECE = ((3, 2, 1, 0), (2, 0, 3, 1), (1, 3, 0, 2), (0, 1, 2, 3))
FAR = [(0, 1), (3, 2)]
NEAR = [(1, 2), (2, 1)]
SECOND = [(0, 2), (3, 1), (1, 0), (2, 3)]
THIRD = [(0, 1), (3, 2), (1, 3), (2, 0)]
MERGE = (0, 1, 2, 0)
KEYS = ((0, 1, 2, 3), (9, 2, 1, 9), (1, 3, 0, 2))
LAST_IN_FRONT = (0, 1, 0, 1)


def gelu(x):
    c = 0.7978845608028654
    half = 0.5 * x
    return half + half * jnp.tanh(x * (c + (c * 0.044715) * (x * x)))


def pair_weights(w_ref):
    zero = jnp.zeros((w_ref.shape[2], w_ref.shape[3]), w_ref.dtype)
    blocks = []
    for j in range(4):
        for d in range(3):
            first = w_ref[j, d] if j < 3 else zero
            second = w_ref[j - 1, d] if j > 0 else zero
            blocks.append(jnp.concatenate([first, second], axis=1))
    return jnp.concatenate(blocks, axis=0)


def odd_row():
    return lax.rem(lax.axis_index("rows"), 2) == 1


def edges_kernel(x_hbm, one_ref, two_ref, sem):
    rows = x_hbm.shape[2]

    def send(near, far):
        a = pltpu.make_async_copy(x_hbm.at[:, :, pl.ds(near, 2)], one_ref, sem.at[0])
        b = pltpu.make_async_copy(x_hbm.at[:, :, pl.ds(far, 2)], two_ref, sem.at[1])
        a.start()
        b.start()
        a.wait()
        b.wait()

    pl.when(odd_row())(functools.partial(send, 0, rows - 2))
    pl.when(jnp.logical_not(odd_row()))(functools.partial(send, rows - 2, 0))


def edges(x):
    planes, cols, rows, ch = x.shape
    shape = jax.ShapeDtypeStruct((planes, cols, 2, ch), x.dtype)
    return pl.pallas_call(
        edges_kernel,
        out_shape=(shape, shape),
        in_specs=[HBM],
        out_specs=(VM, VM),
        scratch_shapes=[pltpu.SemaphoreType.DMA((2,))],
        compiler_params=pltpu.CompilerParams(vmem_limit_bytes=8 << 20),
    )(pltpu.with_memory_space_constraint(x, pltpu.HBM))


def first_conv(xs, w1_ref, bias, c0, cols, emit):
    blocks, wide, ext, ch = xs.shape[1:]
    count = wide - 2
    weights = pair_weights(w1_ref)
    cuts = [count // 2 * i // 2 for i in range(2 + 1)]
    for p, lo, hi in [(p, a, b) for p in range(blocks) for a, b in zip(cuts, cuts[1:])]:
        taps = []
        for j in range(4):
            for d in range(3):
                taps.append(jnp.concatenate([xs[d, p, 2 * g + j] for g in range(lo, hi)], axis=0))
        y = jnp.dot(jnp.concatenate(taps, axis=1), weights, preferred_element_type=F32)
        for c in range(2 * lo, 2 * hi):
            g, o = divmod(c - 2 * lo, 2)
            v = gelu(y[g * ext : (g + 1) * ext, o * ch : (o + 1) * ch] + bias)
            if c == 0:
                v = v * jnp.where(c0 > 0, 1.0, 0.0)
            if c == count - 1:
                v = v * jnp.where(c0 + count - 2 < cols, 1.0, 0.0)
            emit(p, c, v)


def row_masks():
    here = lax.axis_index("rows")
    above = jnp.where(here == 0, 0.0, 1.0)
    below = jnp.where(here == lax.axis_size("rows") - 1, 0.0, 1.0)
    return above, below


def column(c0, c, cols):
    at = c0 - 2 + c
    inside = jnp.logical_and(at >= 0, at < cols)
    return jnp.clip(at, 0, cols - 1), jnp.where(inside, 1.0, 0.0)


def halo_rows(one_ref, two_ref, p, at, odd):
    one = one_ref[p, at].astype(F32)
    two = two_ref[p, at].astype(F32)
    return jnp.where(odd, one, two), jnp.where(odd, two, one)


def second_half(hs, fs, w2_ref, par_ref, out_ref, trans_ref):
    planes, nc, rows, ch = fs.shape
    bias = par_ref[1:2]
    opacity = par_ref[2:3]
    lane = lax.broadcasted_iota(jnp.int32, (rows, ch), 1)
    weights = pair_weights(w2_ref)
    through = jnp.zeros((rows, ch), F32)
    cuts = [nc // 2 * i // 4 for i in range(4 + 1)]
    for lo, hi in zip(cuts, cuts[1:]):
        logits = [jnp.zeros((rows, ch), F32) for _ in range(planes)]
        taps = []
        for j in range(4):
            for d in range(3):
                cells = [hs[d, p, 2 * g + j] for g in range(lo, hi) for p in range(planes)]
                taps.append(jnp.concatenate(cells, axis=0))
        y = jnp.dot(jnp.concatenate(taps, axis=1), weights, preferred_element_type=F32)
        for c in range(2 * lo, 2 * hi):
            g, o = divmod(c - 2 * lo, 2)
            for p in range(planes):
                r0 = (g * planes + p) * rows
                f = gelu(y[r0 : r0 + rows, o * ch : (o + 1) * ch] + bias)
                total = jnp.sum(f * opacity, axis=1, keepdims=True)
                logits[p] = jnp.where(lane == c, total, logits[p])
                fs[p, c] = f
        parts = []
        trans = None
        for p in range(planes):
            alpha = 1.0 / (1.0 + jnp.exp(-(logits[p] + par_ref[3 + p : 4 + p])))
            if p == 0:
                parts.append(alpha)
                trans = 1.0 - alpha
            else:
                parts.append(trans * alpha)
                trans = trans * (1.0 - alpha)
        for c in range(2 * lo, 2 * hi):
            color = sum(parts[p][:, c : c + 1] * fs[p, c] for p in range(planes))
            if trans_ref is None:
                out_ref[c * rows : (c + 1) * rows] = color.astype(BF16)
            else:
                out_ref[c] = color
        mine = jnp.logical_and(lane >= 2 * lo, lane < 2 * hi)
        through = jnp.where(mine, trans, through)
    if trans_ref is None:
        out_ref[nc * rows :] = pack_trans(through, nc)
    else:
        trans_ref[...] = through


def outputs(nc, rows, ch, packed):
    if packed:
        return [jax.ShapeDtypeStruct((nc * rows + rows // folds(nc, rows, ch), ch), BF16)]
    return [jax.ShapeDtypeStruct((nc, rows, ch), F32), jax.ShapeDtypeStruct((rows, ch), F32)]


def call(kernel, args, in_specs, out_shape, scratch):
    return pl.pallas_call(
        kernel,
        out_shape=out_shape,
        in_specs=in_specs,
        out_specs=[VM] * len(out_shape),
        scratch_shapes=scratch,
        compiler_params=pltpu.CompilerParams(vmem_limit_bytes=16 << 20),
        cost_estimate=pl.CostEstimate(flops=5 * 10**9, transcendentals=0, bytes_accessed=10**6),
    )(*args)


def chunk_kernel(pick, packed, x_ref, one_ref, two_ref, w1_ref, w2_ref, par_ref, *refs):
    refs = list(refs)
    out_ref = refs.pop(0)
    trans_ref = None if packed else refs.pop(0)
    f_ref, xs, f2_ref, hs, fs = refs
    planes, cols, rows, ch = x_ref.shape
    nc = fs.shape[1]
    ext = xs.shape[3]
    gap = rows + 8
    c0 = pick() * nc
    odd = odd_row()
    for c in range(nc + 4):
        at, keep = column(c0, c, cols)
        f = f_ref.at[c % f_ref.shape[0]]
        for p in range(planes):
            upper, lower = halo_rows(one_ref, two_ref, p, at, odd)
            r0 = 8 + p * gap
            f[r0 : r0 + rows] = x_ref[p, at].astype(F32) * keep
            f[r0 - 2 : r0] = upper * keep
            f[r0 + rows : r0 + rows + 2] = lower * keep
        for d in range(3):
            xs[d, 0, c] = f[6 + d : 6 + d + ext].astype(BF16)
    above, below = row_masks()

    def emit(_, c, v):
        f2 = f2_ref.at[c]
        f2[...] = v
        for p in range(planes):
            r0 = p * gap
            f2[r0 : r0 + 1] = f2[r0 : r0 + 1] * above
            f2[r0 + rows + 1 : r0 + rows + 2] = f2[r0 + rows + 1 : r0 + rows + 2] * below
            for d in range(3):
                hs[d, p, c] = f2[r0 + d : r0 + d + rows].astype(BF16)

    first_conv(xs, w1_ref, par_ref[0:1], c0, cols, emit)
    second_half(hs, fs, w2_ref, par_ref, out_ref, trans_ref)


def chunk(pick, nc, packed, x, one, two, w1, w2, par):
    planes, cols, rows, ch = x.shape
    ext = -(-((planes - 1) * (rows + 8) + rows + 2) // 16) * 16
    scratch = [
        pltpu.VMEM((4, ext + 16, ch), F32),
        pltpu.VMEM((3, 1, nc + 4, ext, ch), BF16),
        pltpu.VMEM((nc + 2, ext, ch), F32),
        pltpu.VMEM((3, planes, nc + 2, rows, ch), BF16),
        pltpu.VMEM((planes, nc, rows, ch), F32),
    ]
    kernel = functools.partial(chunk_kernel, pick, packed)
    args = (x, one, two, w1, w2, par)
    return call(kernel, args, [VM] * 6, outputs(nc, rows, ch, packed), scratch)


def head_kernel(pick, nc, x_ref, w1_hbm, w2_hbm, b1_hbm, b2_hbm, ow_hbm, ob_ref, *refs):
    hid_ref, w1_ref, w2_ref, par_ref, f_ref, xs, sem = refs
    planes, cols, rows, ch = x_ref.shape
    pairs = [
        (w1_hbm, w1_ref),
        (b1_hbm, par_ref.at[0]),
        (w2_hbm, w2_ref),
        (b2_hbm, par_ref.at[1]),
        (ow_hbm, par_ref.at[2]),
    ]
    copies = [pltpu.make_async_copy(src, dst, sem.at[i]) for i, (src, dst) in enumerate(pairs)]
    for copy in copies:
        copy.start()
    for p in range(planes):
        par_ref[3 + p : 4 + p] = jnp.full((1, ch), ob_ref[p])
    c0 = pick() * nc
    for i in range(planes * (nc + 4)):
        p, c = divmod(i, nc + 4)
        at, keep = column(c0, c, cols)
        f = f_ref.at[i % f_ref.shape[0]]
        f[16 : 16 + rows] = x_ref[p, at].astype(F32) * keep
        for d in range(3):
            xs[d, p, c] = f[15 + d : 15 + d + rows].astype(BF16)
    copies[0].wait()
    copies[1].wait()

    def emit(p, c, v):
        hid_ref[p, c, 8 : 8 + rows] = v

    first_conv(xs, w1_ref, par_ref[0:1], c0, cols, emit)
    for copy in copies[2:]:
        copy.wait()


def head(pick, nc, x, w1, w2, b1, b2, ow, ob):
    planes, cols, rows, ch = x.shape
    args = [pltpu.with_memory_space_constraint(a, pltpu.HBM) for a in (w1, w2, b1, b2, ow)]
    out_shape = [
        jax.ShapeDtypeStruct((planes, nc + 2, rows + 16, ch), F32),
        jax.ShapeDtypeStruct(w1.shape, w1.dtype),
        jax.ShapeDtypeStruct(w2.shape, w2.dtype),
        jax.ShapeDtypeStruct((3 + planes, ch), F32),
    ]
    scratch = [
        pltpu.VMEM((8, rows + 32, ch), F32),
        pltpu.VMEM((3, planes, nc + 4, rows, ch), BF16),
        pltpu.SemaphoreType.DMA((5,)),
    ]
    in_specs = [VM] + [HBM] * 5 + [pl.BlockSpec(memory_space=pltpu.SMEM)]
    kernel = functools.partial(head_kernel, pick, nc)
    return call(kernel, (x, *args, ob), in_specs, out_shape, scratch)


def tail_kernel(pick, x_ref, one_ref, two_ref, hid_ref, w1_ref, w2_ref, par_ref, out_ref, *refs):
    f_ref, xs, edge_ref, f2_ref, hs, fs = refs
    planes, cols, rows, ch = x_ref.shape
    nc = fs.shape[1]
    c0 = pick() * nc
    odd = odd_row()
    for i in range(planes * (nc + 4)):
        p, c = divmod(i, nc + 4)
        at, keep = column(c0, c, cols)
        f = f_ref.at[i % f_ref.shape[0]]
        upper, lower = halo_rows(one_ref, two_ref, p, at, odd)
        f[6:8] = upper * keep
        f[8:16] = x_ref[p, at, 0:8].astype(F32) * keep
        f[24:32] = x_ref[p, at, rows - 8 : rows].astype(F32) * keep
        f[32:34] = lower * keep
        for d in range(3):
            both = jnp.concatenate([f[3 + d : 11 + d], f[27 + d : 35 + d]], axis=0)
            xs[d, p, c] = both.astype(BF16)
    above, below = row_masks()

    def emit(p, c, v):
        edge = edge_ref.at[p, c]
        edge[...] = v
        f2 = f2_ref.at[p, c]
        f2[8 : 8 + rows] = hid_ref[p, c, 8 : 8 + rows]
        f2[7:8] = edge[3:4] * above
        f2[8:9] = edge[4:5]
        f2[7 + rows : 8 + rows] = edge[11:12]
        f2[8 + rows : 9 + rows] = edge[12:13] * below
        for d in range(3):
            hs[d, p, c] = f2[7 + d : 7 + d + rows].astype(BF16)

    first_conv(xs, w1_ref, par_ref[0:1], c0, cols, emit)
    second_half(hs, fs, w2_ref, par_ref, out_ref, None)


def tail(pick, nc, x, one, two, hid, w1, w2, par):
    planes, cols, rows, ch = x.shape
    scratch = [
        pltpu.VMEM((8, 40, ch), F32),
        pltpu.VMEM((3, planes, nc + 4, 16, ch), BF16),
        pltpu.VMEM((planes, nc + 2, 16, ch), F32),
        pltpu.VMEM((planes, nc + 2, rows + 16, ch), F32),
        pltpu.VMEM((3, planes, nc + 2, rows, ch), BF16),
        pltpu.VMEM((planes, nc, rows, ch), F32),
    ]
    args = (x, one, two, hid, w1, w2, par)
    kernel = functools.partial(tail_kernel, pick)
    return call(kernel, args, [VM] * 7, outputs(nc, rows, ch, True), scratch)[0]


def lookup(table):
    here = lax.axis_index("depth")
    value = jnp.int32(table[-1])
    for i in range(len(table) - 1):
        value = jnp.where(here == i, table[i], value)
    return value


def folds(nc, rows, ch):
    return min(rows // 16, ch // (2 * nc))


def unpack_trans(ref, nc, rows):
    ch = ref.shape[1]
    fold = folds(nc, rows, ch)
    block = ref[nc * rows :].astype(F32)
    block = block + pltpu.roll(block, ch - nc, axis=1)
    parts = [block] + [pltpu.roll(block, ch - 2 * nc * q, axis=1) for q in range(1, fold)]
    return jnp.concatenate(parts, axis=0)


def pack_trans(trans, nc):
    rows, ch = trans.shape
    fold = folds(nc, rows, ch)
    size = rows // fold
    lane = lax.broadcasted_iota(jnp.int32, trans.shape, 1)
    high = trans.astype(BF16).astype(F32)
    low = pltpu.roll(trans - high, nc, axis=1)
    both = jnp.where(lane < nc, high, jnp.where(lane < 2 * nc, low, 0.0))
    block = both[:size]
    for q in range(1, fold):
        block = block + pltpu.roll(both[q * size : (q + 1) * size], 2 * nc * q, axis=1)
    return block.astype(BF16)


def merge_kernel(own_ref, trans_ref, got_ref, out_ref):
    nc = own_ref.shape[0]
    mine = trans_ref[...]
    rows = own_ref.shape[1]
    theirs = unpack_trans(got_ref, nc, rows)
    role = lookup(MERGE)
    scale_own = jnp.where(role == 1, theirs, 1.0)
    scale_got = jnp.where(role == 2, mine, jnp.where(role == 1, 1.0, 0.0))
    for c in range(nc):
        color = scale_own[:, c : c + 1] * own_ref[c]
        at = slice(c * rows, (c + 1) * rows)
        color = color + scale_got[:, c : c + 1] * got_ref[at].astype(F32)
        out_ref[at] = color.astype(BF16)
    out_ref[nc * rows :] = pack_trans(jnp.where(role == 0, mine, mine * theirs), nc)


def merge(own, trans, got):
    return pl.pallas_call(
        merge_kernel,
        out_shape=jax.ShapeDtypeStruct(got.shape, BF16),
        in_specs=[VM] * 3,
        out_specs=VM,
        compiler_params=pltpu.CompilerParams(vmem_limit_bytes=8 << 20),
        cost_estimate=pl.CostEstimate(flops=10**9, transcendentals=0, bytes_accessed=10**6),
    )(own, trans, got)


def gather_kernel(own_ref, trans_ref, *refs):
    *got_refs, out_ref, out_trans_ref = refs
    nc, rows = own_ref.shape[:2]
    keys = [lookup(table) for table in KEYS]
    trans = [trans_ref[...]] + [unpack_trans(ref, nc, rows) for ref in got_refs]
    scale = []
    through = None
    for k in range(len(trans)):
        w = None
        for m in range(len(trans)):
            if m != k:
                term = jnp.where(keys[m] < keys[k], trans[m], 1.0)
                w = term if w is None else w * term
        scale.append(w)
        term = jnp.where(keys[k] == 9, 1.0, trans[k])
        through = term if through is None else through * term
    for c in range(nc):
        total = scale[0][:, c : c + 1] * own_ref[c]
        for k, ref in enumerate(got_refs):
            at = slice(c * rows, (c + 1) * rows)
            total = total + scale[k + 1][:, c : c + 1] * ref[at].astype(F32)
        out_ref[c] = total
    out_trans_ref[...] = through


def finish_kernel(near_ref, trans_ref, got_ref, out_hbm, out, sem):
    nc, rows = near_ref.shape[:2]
    front = lookup(LAST_IN_FRONT) == 1
    theirs = unpack_trans(got_ref, nc, rows)
    scale_near = jnp.where(front, theirs, 1.0)
    scale_got = jnp.where(front, 1.0, trans_ref[...])
    pieces = sem.shape[0]
    step = nc // pieces
    copies = []
    for i in range(pieces):
        for c in range(i * step, (i + 1) * step):
            got = got_ref[c * rows : (c + 1) * rows].astype(F32)
            out[c] = scale_near[:, c : c + 1] * near_ref[c] + scale_got[:, c : c + 1] * got
        at = pl.ds(i * step, step)
        copies.append(pltpu.make_async_copy(out.at[at], out_hbm.at[at], sem.at[i]))
        copies[-1].start()
    for copy in copies:
        copy.wait()


def combine(own, trans, got):
    color = jax.ShapeDtypeStruct(own.shape, F32)
    near, trans = pl.pallas_call(
        gather_kernel,
        out_shape=[color, jax.ShapeDtypeStruct(trans.shape, F32)],
        in_specs=[VM] * 4,
        out_specs=[VM] * 2,
        compiler_params=pltpu.CompilerParams(vmem_limit_bytes=8 << 20),
        cost_estimate=pl.CostEstimate(flops=10**9, transcendentals=0, bytes_accessed=10**6),
    )(own, trans, *got[:2])
    return pl.pallas_call(
        finish_kernel,
        out_shape=color,
        in_specs=[VM] * 3,
        out_specs=HBM,
        scratch_shapes=[pltpu.VMEM(own.shape, F32), pltpu.SemaphoreType.DMA((4,))],
        compiler_params=pltpu.CompilerParams(vmem_limit_bytes=8 << 20),
    )(near, trans, got[2])


def exchange(value, axis, mask):
    pairs = [(i, i ^ mask) for i in range(lax.axis_size(axis))]
    return lax.ppermute(value, axis, pairs)


def pick_half(array, remaining, bit_set):
    shaped = array.reshape((remaining // 2, 2, -1) + array.shape[1:])
    first_half = shaped[:, 0].reshape((-1,) + array.shape[1:])
    second_half = shaped[:, 1].reshape((-1,) + array.shape[1:])
    keep = jnp.where(bit_set, second_half, first_half)
    other = jnp.where(bit_set, first_half, second_half)
    return (keep, other)


def butterfly(color, trans):
    position = lax.axis_index("depth")
    slabs = lax.axis_size("depth")
    for level in range(slabs.bit_length() - 1):
        remaining = slabs >> level
        bit_set = jnp.right_shift(position, level) % 2 == 1
        keep_color, send_color = pick_half(color, remaining, bit_set)
        keep_trans, send_trans = pick_half(trans, remaining, bit_set)
        got_color = exchange(send_color, "depth", 2**level)
        got_trans = exchange(send_trans, "depth", 2**level)
        color = jnp.where(
            bit_set,
            got_color + got_trans[..., None] * keep_color,
            keep_color + keep_trans[..., None] * got_color,
        )
        trans = keep_trans * got_trans
    return color


def per_device(volume, conv_one, bias_one, conv_two, bias_two, opacity_weight, opacity_bias):
    planes, cols, rows, ch = volume.shape
    slabs = lax.axis_size("depth")
    size = lax.axis_size("rows")
    one, two = edges(volume)
    one = lax.ppermute(one, "rows", [(i, i ^ 1) for i in range(size)])
    inner = [(i, i + 1) for i in range(1, size - 1, 2)]
    two = lax.ppermute(two, "rows", inner + [(j, i) for i, j in inner])
    if slabs != 4:
        par = jnp.concatenate(
            [
                jnp.stack([bias_one, bias_two, opacity_weight]),
                jnp.broadcast_to(opacity_bias[:, None], (planes, ch)),
            ]
        )
        args = (16, False, volume, one, two, conv_one, conv_two, par)
        done = [chunk(functools.partial(jnp.int32, i), *args) for i in range(cols // 16)]
        color = jnp.concatenate([c for c, _ in done])
        trans = jnp.concatenate([jnp.transpose(t[:, :16]) for _, t in done])
        return butterfly(color, trans)
    nc = cols // slabs
    picks = [functools.partial(lookup, [order[slot] for order in PIECE]) for slot in range(4)]
    hid, w1, w2, par = head(
        picks[0], nc, volume, conv_one, conv_two, bias_one, bias_two, opacity_weight, opacity_bias
    )

    def piece(slot, packed):
        return chunk(picks[slot], nc, packed, volume, one, two, w1, w2, par)

    first = tail(picks[0], nc, volume, one, two, hid, w1, w2, par)
    far = lax.ppermute(first, "depth", FAR)
    near = lax.ppermute(first, "depth", NEAR)
    (second,) = piece(1, True)
    second = lax.ppermute(second, "depth", SECOND)
    third = lax.ppermute(merge(*piece(2, False), far), "depth", THIRD)
    own, trans = piece(3, False)
    return combine(own, trans, [near, second, third])


def solution(mesh):
    in_specs = (P(("grp", "depth"), None, "rows", None), P(), P(), P(), P(), P(), P("depth"))
    out_specs = P(("grp", "depth"), "rows", None)
    return jax.shard_map(
        per_device, mesh=mesh, in_specs=in_specs, out_specs=out_specs, check_vma=False
    )
```

```python
import functools

import jax
import jax.numpy as jnp
from jax import lax
from jax.experimental import pallas as pl
from jax.experimental.pallas import tpu as pltpu
from jax.sharding import PartitionSpec as P

VM = pl.BlockSpec(memory_space=pltpu.VMEM)
HBM = pl.BlockSpec(memory_space=pltpu.HBM)
F32 = jnp.float32
BF16 = jnp.bfloat16

PIECE = ((3, 2, 1, 0), (2, 0, 3, 1), (1, 3, 0, 2), (0, 1, 2, 3))
FAR = [(0, 1), (3, 2)]
NEAR = [(1, 2), (2, 1)]
SECOND = [(0, 2), (3, 1), (1, 0), (2, 3)]
THIRD = [(0, 1), (3, 2), (1, 3), (2, 0)]
MERGE = (0, 1, 2, 0)
KEYS = ((0, 1, 2, 3), (9, 2, 1, 9), (1, 3, 0, 2))
LAST_IN_FRONT = (0, 1, 0, 1)


def gelu(x):
    c = 0.7978845608028654
    half = 0.5 * x
    return half + half * jnp.tanh(x * (c + (c * 0.044715) * (x * x)))


def pair_weights(w_ref):
    zero = jnp.zeros((w_ref.shape[2], w_ref.shape[3]), w_ref.dtype)
    blocks = []
    for j in range(4):
        for d in range(3):
            first = w_ref[j, d] if j < 3 else zero
            second = w_ref[j - 1, d] if j > 0 else zero
            blocks.append(jnp.concatenate([first, second], axis=1))
    return jnp.concatenate(blocks, axis=0)


def odd_row():
    return lax.rem(lax.axis_index("rows"), 2) == 1


def edges_kernel(x_hbm, w_hbm, b_hbm, one_ref, two_ref, w_ref, b_ref, sem):
    rows = x_hbm.shape[2]
    weights = pltpu.make_async_copy(w_hbm, w_ref, sem.at[2])
    bias = pltpu.make_async_copy(b_hbm, b_ref.at[0], sem.at[3])

    def send(near, far):
        a = pltpu.make_async_copy(x_hbm.at[:, :, pl.ds(near, 2)], one_ref, sem.at[0])
        b = pltpu.make_async_copy(x_hbm.at[:, :, pl.ds(far, 2)], two_ref, sem.at[1])
        a.start()
        b.start()
        weights.start()
        bias.start()
        a.wait()
        b.wait()
        weights.wait()
        bias.wait()

    pl.when(odd_row())(functools.partial(send, 0, rows - 2))
    pl.when(jnp.logical_not(odd_row()))(functools.partial(send, rows - 2, 0))


def edges(x, w, b):
    planes, cols, rows, ch = x.shape
    shape = jax.ShapeDtypeStruct((planes, cols, 2, ch), x.dtype)
    return pl.pallas_call(
        edges_kernel,
        out_shape=(
            shape,
            shape,
            jax.ShapeDtypeStruct(w.shape, w.dtype),
            jax.ShapeDtypeStruct((1, ch), F32),
        ),
        in_specs=[HBM] * 3,
        out_specs=(VM,) * 4,
        scratch_shapes=[pltpu.SemaphoreType.DMA((4,))],
        compiler_params=pltpu.CompilerParams(vmem_limit_bytes=8 << 20),
    )(*[pltpu.with_memory_space_constraint(a, pltpu.HBM) for a in (x, w, b)])


def first_conv(xs, w1_ref, bias, c0, cols, emit):
    blocks, wide, ext, ch = xs.shape[1:]
    count = wide - 2
    weights = pair_weights(w1_ref)
    cuts = [count // 2 * i // 2 for i in range(2 + 1)]
    for p, lo, hi in [(p, a, b) for p in range(blocks) for a, b in zip(cuts, cuts[1:])]:
        taps = []
        for j in range(4):
            for d in range(3):
                taps.append(jnp.concatenate([xs[d, p, 2 * g + j] for g in range(lo, hi)], axis=0))
        y = jnp.dot(jnp.concatenate(taps, axis=1), weights, preferred_element_type=F32)
        for c in range(2 * lo, 2 * hi):
            g, o = divmod(c - 2 * lo, 2)
            v = gelu(y[g * ext : (g + 1) * ext, o * ch : (o + 1) * ch] + bias)
            if c == 0:
                v = v * jnp.where(c0 > 0, 1.0, 0.0)
            if c == count - 1:
                v = v * jnp.where(c0 + count - 2 < cols, 1.0, 0.0)
            emit(p, c, v)


def row_masks():
    here = lax.axis_index("rows")
    above = jnp.where(here == 0, 0.0, 1.0)
    below = jnp.where(here == lax.axis_size("rows") - 1, 0.0, 1.0)
    return above, below


def column(c0, c, cols):
    at = c0 - 2 + c
    inside = jnp.logical_and(at >= 0, at < cols)
    return jnp.clip(at, 0, cols - 1), jnp.where(inside, 1.0, 0.0)


def halo_rows(one_ref, two_ref, p, at, odd):
    one = one_ref[p, at].astype(F32)
    two = two_ref[p, at].astype(F32)
    return jnp.where(odd, one, two), jnp.where(odd, two, one)


def second_half(hs, fs, w2_ref, par_ref, out_ref, trans_ref):
    planes, nc, rows, ch = fs.shape
    bias = par_ref[1:2]
    opacity = par_ref[2:3]
    lane = lax.broadcasted_iota(jnp.int32, (rows, ch), 1)
    weights = pair_weights(w2_ref)
    through = jnp.zeros((rows, ch), F32)
    cuts = [nc // 2 * i // 4 for i in range(4 + 1)]
    for lo, hi in zip(cuts, cuts[1:]):
        logits = [jnp.zeros((rows, ch), F32) for _ in range(planes)]
        taps = []
        for j in range(4):
            for d in range(3):
                cells = [hs[d, p, 2 * g + j] for g in range(lo, hi) for p in range(planes)]
                taps.append(jnp.concatenate(cells, axis=0))
        y = jnp.dot(jnp.concatenate(taps, axis=1), weights, preferred_element_type=F32)
        for c in range(2 * lo, 2 * hi):
            g, o = divmod(c - 2 * lo, 2)
            for p in range(planes):
                r0 = (g * planes + p) * rows
                f = gelu(y[r0 : r0 + rows, o * ch : (o + 1) * ch] + bias)
                total = jnp.sum(f * opacity, axis=1, keepdims=True)
                logits[p] = jnp.where(lane == c, total, logits[p])
                fs[p, c] = f
        parts = []
        trans = None
        for p in range(planes):
            alpha = 1.0 / (1.0 + jnp.exp(-(logits[p] + par_ref[3 + p : 4 + p])))
            if p == 0:
                parts.append(alpha)
                trans = 1.0 - alpha
            else:
                parts.append(trans * alpha)
                trans = trans * (1.0 - alpha)
        for c in range(2 * lo, 2 * hi):
            color = sum(parts[p][:, c : c + 1] * fs[p, c] for p in range(planes))
            if trans_ref is None:
                out_ref[c * rows : (c + 1) * rows] = color.astype(BF16)
            else:
                out_ref[c] = color
        mine = jnp.logical_and(lane >= 2 * lo, lane < 2 * hi)
        through = jnp.where(mine, trans, through)
    if trans_ref is None:
        out_ref[nc * rows :] = pack_trans(through, nc)
    else:
        trans_ref[...] = through


def outputs(nc, rows, ch, packed):
    if packed:
        return [jax.ShapeDtypeStruct((nc * rows + rows // folds(nc, rows, ch), ch), BF16)]
    return [jax.ShapeDtypeStruct((nc, rows, ch), F32), jax.ShapeDtypeStruct((rows, ch), F32)]


def call(kernel, args, in_specs, out_shape, scratch):
    return pl.pallas_call(
        kernel,
        out_shape=out_shape,
        in_specs=in_specs,
        out_specs=[VM] * len(out_shape),
        scratch_shapes=scratch,
        compiler_params=pltpu.CompilerParams(vmem_limit_bytes=16 << 20),
        cost_estimate=pl.CostEstimate(flops=5 * 10**9, transcendentals=0, bytes_accessed=10**6),
    )(*args)


def chunk_kernel(pick, packed, x_ref, one_ref, two_ref, w1_ref, w2_ref, par_ref, *refs):
    refs = list(refs)
    out_ref = refs.pop(0)
    trans_ref = None if packed else refs.pop(0)
    f_ref, xs, f2_ref, hs, fs = refs
    planes, cols, rows, ch = x_ref.shape
    nc = fs.shape[1]
    ext = xs.shape[3]
    gap = rows + 8
    c0 = pick() * nc
    odd = odd_row()
    for c in range(nc + 4):
        at, keep = column(c0, c, cols)
        f = f_ref.at[c % f_ref.shape[0]]
        for p in range(planes):
            upper, lower = halo_rows(one_ref, two_ref, p, at, odd)
            r0 = 8 + p * gap
            f[r0 : r0 + rows] = x_ref[p, at].astype(F32) * keep
            f[r0 - 2 : r0] = upper * keep
            f[r0 + rows : r0 + rows + 2] = lower * keep
        for d in range(3):
            xs[d, 0, c] = f[6 + d : 6 + d + ext].astype(BF16)
    above, below = row_masks()

    def emit(_, c, v):
        f2 = f2_ref.at[c]
        f2[...] = v
        for p in range(planes):
            r0 = p * gap
            f2[r0 : r0 + 1] = f2[r0 : r0 + 1] * above
            f2[r0 + rows + 1 : r0 + rows + 2] = f2[r0 + rows + 1 : r0 + rows + 2] * below
            for d in range(3):
                hs[d, p, c] = f2[r0 + d : r0 + d + rows].astype(BF16)

    first_conv(xs, w1_ref, par_ref[0:1], c0, cols, emit)
    second_half(hs, fs, w2_ref, par_ref, out_ref, trans_ref)


def chunk(pick, nc, packed, x, one, two, w1, w2, par):
    planes, cols, rows, ch = x.shape
    ext = -(-((planes - 1) * (rows + 8) + rows + 2) // 16) * 16
    scratch = [
        pltpu.VMEM((4, ext + 16, ch), F32),
        pltpu.VMEM((3, 1, nc + 4, ext, ch), BF16),
        pltpu.VMEM((nc + 2, ext, ch), F32),
        pltpu.VMEM((3, planes, nc + 2, rows, ch), BF16),
        pltpu.VMEM((planes, nc, rows, ch), F32),
    ]
    kernel = functools.partial(chunk_kernel, pick, packed)
    args = (x, one, two, w1, w2, par)
    return call(kernel, args, [VM] * 6, outputs(nc, rows, ch, packed), scratch)


def head_kernel(pick, nc, x_ref, w1_ref, b1_ref, w2_hbm, b2_hbm, ow_hbm, ob_ref, *refs):
    hid_ref, w2_ref, par_ref, f_ref, xs, sem = refs
    planes, cols, rows, ch = x_ref.shape
    pairs = [
        (w2_hbm, w2_ref),
        (b2_hbm, par_ref.at[1]),
        (ow_hbm, par_ref.at[2]),
    ]
    copies = [pltpu.make_async_copy(src, dst, sem.at[i]) for i, (src, dst) in enumerate(pairs)]
    for copy in copies:
        copy.start()
    par_ref[3:] = ob_ref[...]
    c0 = pick() * nc
    for i in range(planes * (nc + 4)):
        p, c = divmod(i, nc + 4)
        at, keep = column(c0, c, cols)
        f = f_ref.at[i % f_ref.shape[0]]
        f[16 : 16 + rows] = x_ref[p, at].astype(F32) * keep
        for d in range(3):
            xs[d, p, c] = f[15 + d : 15 + d + rows].astype(BF16)
    par_ref[0:1] = b1_ref[...]

    def emit(p, c, v):
        hid_ref[p, c, 8 : 8 + rows] = v

    first_conv(xs, w1_ref, b1_ref[...], c0, cols, emit)
    for copy in copies:
        copy.wait()


def head(pick, nc, x, w1, w2, b1, b2, ow, ob):
    planes, cols, rows, ch = x.shape
    args = [pltpu.with_memory_space_constraint(a, pltpu.HBM) for a in (w2, b2, ow)]
    out_shape = [
        jax.ShapeDtypeStruct((planes, nc + 2, rows + 16, ch), F32),
        jax.ShapeDtypeStruct(w2.shape, w2.dtype),
        jax.ShapeDtypeStruct((3 + planes, ch), F32),
    ]
    scratch = [
        pltpu.VMEM((8, rows + 32, ch), F32),
        pltpu.VMEM((3, planes, nc + 4, rows, ch), BF16),
        pltpu.SemaphoreType.DMA((3,)),
    ]
    in_specs = [VM] * 3 + [HBM] * 3 + [VM]
    kernel = functools.partial(head_kernel, pick, nc)
    return call(kernel, (x, w1, b1, *args, ob), in_specs, out_shape, scratch)


def tail_kernel(pick, x_ref, one_ref, two_ref, hid_ref, w1_ref, w2_ref, par_ref, out_ref, *refs):
    f_ref, xs, edge_ref, f2_ref, hs, fs = refs
    planes, cols, rows, ch = x_ref.shape
    nc = fs.shape[1]
    c0 = pick() * nc
    odd = odd_row()
    for i in range(planes * (nc + 4)):
        p, c = divmod(i, nc + 4)
        at, keep = column(c0, c, cols)
        f = f_ref.at[i % f_ref.shape[0]]
        upper, lower = halo_rows(one_ref, two_ref, p, at, odd)
        f[6:8] = upper * keep
        f[8:16] = x_ref[p, at, 0:8].astype(F32) * keep
        f[24:32] = x_ref[p, at, rows - 8 : rows].astype(F32) * keep
        f[32:34] = lower * keep
        for d in range(3):
            both = jnp.concatenate([f[3 + d : 11 + d], f[27 + d : 35 + d]], axis=0)
            xs[d, p, c] = both.astype(BF16)
    above, below = row_masks()

    def emit(p, c, v):
        edge = edge_ref.at[p, c]
        edge[...] = v
        f2 = f2_ref.at[p, c]
        f2[8 : 8 + rows] = hid_ref[p, c, 8 : 8 + rows]
        f2[7:8] = edge[3:4] * above
        f2[8:9] = edge[4:5]
        f2[7 + rows : 8 + rows] = edge[11:12]
        f2[8 + rows : 9 + rows] = edge[12:13] * below
        for d in range(3):
            hs[d, p, c] = f2[7 + d : 7 + d + rows].astype(BF16)

    first_conv(xs, w1_ref, par_ref[0:1], c0, cols, emit)
    second_half(hs, fs, w2_ref, par_ref, out_ref, None)


def tail(pick, nc, x, one, two, hid, w1, w2, par):
    planes, cols, rows, ch = x.shape
    scratch = [
        pltpu.VMEM((8, 40, ch), F32),
        pltpu.VMEM((3, planes, nc + 4, 16, ch), BF16),
        pltpu.VMEM((planes, nc + 2, 16, ch), F32),
        pltpu.VMEM((planes, nc + 2, rows + 16, ch), F32),
        pltpu.VMEM((3, planes, nc + 2, rows, ch), BF16),
        pltpu.VMEM((planes, nc, rows, ch), F32),
    ]
    args = (x, one, two, hid, w1, w2, par)
    kernel = functools.partial(tail_kernel, pick)
    return call(kernel, args, [VM] * 7, outputs(nc, rows, ch, True), scratch)[0]


def lookup(table):
    here = lax.axis_index("depth")
    value = jnp.int32(table[-1])
    for i in range(len(table) - 1):
        value = jnp.where(here == i, table[i], value)
    return value


def folds(nc, rows, ch):
    return min(rows // 16, ch // (2 * nc))


def unpack_trans(ref, nc, rows):
    ch = ref.shape[1]
    fold = folds(nc, rows, ch)
    block = ref[nc * rows :].astype(F32)
    block = block + pltpu.roll(block, ch - nc, axis=1)
    parts = [block] + [pltpu.roll(block, ch - 2 * nc * q, axis=1) for q in range(1, fold)]
    return jnp.concatenate(parts, axis=0)


def pack_trans(trans, nc):
    rows, ch = trans.shape
    fold = folds(nc, rows, ch)
    size = rows // fold
    lane = lax.broadcasted_iota(jnp.int32, trans.shape, 1)
    high = trans.astype(BF16).astype(F32)
    low = pltpu.roll(trans - high, nc, axis=1)
    both = jnp.where(lane < nc, high, jnp.where(lane < 2 * nc, low, 0.0))
    block = both[:size]
    for q in range(1, fold):
        block = block + pltpu.roll(both[q * size : (q + 1) * size], 2 * nc * q, axis=1)
    return block.astype(BF16)


def merge_kernel(own_ref, trans_ref, got_ref, out_ref):
    nc = own_ref.shape[0]
    mine = trans_ref[...]
    rows = own_ref.shape[1]
    theirs = unpack_trans(got_ref, nc, rows)
    role = lookup(MERGE)
    scale_own = jnp.where(role == 1, theirs, 1.0)
    scale_got = jnp.where(role == 2, mine, jnp.where(role == 1, 1.0, 0.0))
    for c in range(nc):
        color = scale_own[:, c : c + 1] * own_ref[c]
        at = slice(c * rows, (c + 1) * rows)
        color = color + scale_got[:, c : c + 1] * got_ref[at].astype(F32)
        out_ref[at] = color.astype(BF16)
    out_ref[nc * rows :] = pack_trans(jnp.where(role == 0, mine, mine * theirs), nc)


def merge(own, trans, got):
    return pl.pallas_call(
        merge_kernel,
        out_shape=jax.ShapeDtypeStruct(got.shape, BF16),
        in_specs=[VM] * 3,
        out_specs=VM,
        compiler_params=pltpu.CompilerParams(vmem_limit_bytes=8 << 20),
        cost_estimate=pl.CostEstimate(flops=10**9, transcendentals=0, bytes_accessed=10**6),
    )(own, trans, got)


def gather_kernel(own_ref, trans_ref, *refs):
    *got_refs, out_ref, out_trans_ref = refs
    nc, rows = own_ref.shape[:2]
    keys = [lookup(table) for table in KEYS]
    trans = [trans_ref[...]] + [unpack_trans(ref, nc, rows) for ref in got_refs]
    scale = []
    through = None
    for k in range(len(trans)):
        w = None
        for m in range(len(trans)):
            if m != k:
                term = jnp.where(keys[m] < keys[k], trans[m], 1.0)
                w = term if w is None else w * term
        scale.append(w)
        term = jnp.where(keys[k] == 9, 1.0, trans[k])
        through = term if through is None else through * term
    for c in range(nc):
        total = scale[0][:, c : c + 1] * own_ref[c]
        for k, ref in enumerate(got_refs):
            at = slice(c * rows, (c + 1) * rows)
            total = total + scale[k + 1][:, c : c + 1] * ref[at].astype(F32)
        out_ref[c] = total
    out_trans_ref[...] = through


def finish_kernel(near_ref, trans_ref, got_ref, out_hbm, out, sem):
    nc, rows = near_ref.shape[:2]
    front = lookup(LAST_IN_FRONT) == 1
    theirs = unpack_trans(got_ref, nc, rows)
    scale_near = jnp.where(front, theirs, 1.0)
    scale_got = jnp.where(front, 1.0, trans_ref[...])
    pieces = sem.shape[0]
    step = nc // pieces
    copies = []
    for i in range(pieces):
        for c in range(i * step, (i + 1) * step):
            got = got_ref[c * rows : (c + 1) * rows].astype(F32)
            out[c] = scale_near[:, c : c + 1] * near_ref[c] + scale_got[:, c : c + 1] * got
        at = pl.ds(i * step, step)
        copies.append(pltpu.make_async_copy(out.at[at], out_hbm.at[at], sem.at[i]))
        copies[-1].start()
    for copy in copies:
        copy.wait()


def combine(own, trans, got):
    color = jax.ShapeDtypeStruct(own.shape, F32)
    near, trans = pl.pallas_call(
        gather_kernel,
        out_shape=[color, jax.ShapeDtypeStruct(trans.shape, F32)],
        in_specs=[VM] * 4,
        out_specs=[VM] * 2,
        compiler_params=pltpu.CompilerParams(vmem_limit_bytes=8 << 20),
        cost_estimate=pl.CostEstimate(flops=10**9, transcendentals=0, bytes_accessed=10**6),
    )(own, trans, *got[:2])
    return pl.pallas_call(
        finish_kernel,
        out_shape=color,
        in_specs=[VM] * 3,
        out_specs=HBM,
        scratch_shapes=[pltpu.VMEM(own.shape, F32), pltpu.SemaphoreType.DMA((4,))],
        compiler_params=pltpu.CompilerParams(vmem_limit_bytes=8 << 20),
    )(near, trans, got[2])


def exchange(value, axis, mask):
    pairs = [(i, i ^ mask) for i in range(lax.axis_size(axis))]
    return lax.ppermute(value, axis, pairs)


def pick_half(array, remaining, bit_set):
    shaped = array.reshape((remaining // 2, 2, -1) + array.shape[1:])
    first_half = shaped[:, 0].reshape((-1,) + array.shape[1:])
    second_half = shaped[:, 1].reshape((-1,) + array.shape[1:])
    keep = jnp.where(bit_set, second_half, first_half)
    other = jnp.where(bit_set, first_half, second_half)
    return (keep, other)


def butterfly(color, trans):
    position = lax.axis_index("depth")
    slabs = lax.axis_size("depth")
    for level in range(slabs.bit_length() - 1):
        remaining = slabs >> level
        bit_set = jnp.right_shift(position, level) % 2 == 1
        keep_color, send_color = pick_half(color, remaining, bit_set)
        keep_trans, send_trans = pick_half(trans, remaining, bit_set)
        got_color = exchange(send_color, "depth", 2**level)
        got_trans = exchange(send_trans, "depth", 2**level)
        color = jnp.where(
            bit_set,
            got_color + got_trans[..., None] * keep_color,
            keep_color + keep_trans[..., None] * got_color,
        )
        trans = keep_trans * got_trans
    return color


def per_device(volume, conv_one, bias_one, conv_two, bias_two, opacity_weight, opacity_bias):
    planes, cols, rows, ch = volume.shape
    slabs = lax.axis_size("depth")
    size = lax.axis_size("rows")
    one, two, w1, b1 = edges(volume, conv_one, bias_one)
    inner = [(i, i + 1) for i in range(1, size - 1, 2)]
    two = lax.ppermute(two, "rows", inner + [(j, i) for i, j in inner])
    one = lax.ppermute(one, "rows", [(i, i ^ 1) for i in range(size)])
    if slabs != 4:
        par = jnp.concatenate(
            [
                jnp.stack([bias_one, bias_two, opacity_weight]),
                jnp.broadcast_to(opacity_bias[:, None], (planes, ch)),
            ]
        )
        args = (16, False, volume, one, two, w1, conv_two, par)
        done = [chunk(functools.partial(jnp.int32, i), *args) for i in range(cols // 16)]
        color = jnp.concatenate([c for c, _ in done])
        trans = jnp.concatenate([jnp.transpose(t[:, :16]) for _, t in done])
        return butterfly(color, trans)
    nc = cols // slabs
    picks = [functools.partial(lookup, [order[slot] for order in PIECE]) for slot in range(4)]
    offsets = jnp.broadcast_to(opacity_bias[:, None], (planes, ch))
    hid, w2, par = head(
        picks[0], nc, volume, w1, conv_two, b1, bias_two, opacity_weight, offsets
    )

    def piece(slot, packed):
        return chunk(picks[slot], nc, packed, volume, one, two, w1, w2, par)

    first = tail(picks[0], nc, volume, one, two, hid, w1, w2, par)
    far = lax.ppermute(first, "depth", FAR)
    near = lax.ppermute(first, "depth", NEAR)
    (second,) = piece(1, True)
    second = lax.ppermute(second, "depth", SECOND)
    third = lax.ppermute(merge(*piece(2, False), far), "depth", THIRD)
    own, trans = piece(3, False)
    return combine(own, trans, [near, second, third])


def solution(mesh):
    in_specs = (P(("grp", "depth"), None, "rows", None), P(), P(), P(), P(), P(), P("depth"))
    out_specs = P(("grp", "depth"), "rows", None)
    return jax.shard_map(
        per_device, mesh=mesh, in_specs=in_specs, out_specs=out_specs, check_vma=False
    )
```

```python
import functools

import jax
import jax.numpy as jnp
from jax import lax
from jax.experimental import pallas as pl
from jax.experimental.pallas import tpu as pltpu
from jax.sharding import PartitionSpec as P

VM = pl.BlockSpec(memory_space=pltpu.VMEM)
HBM = pl.BlockSpec(memory_space=pltpu.HBM)
F32 = jnp.float32
BF16 = jnp.bfloat16

PIECE = ((3, 2, 1, 0), (2, 0, 3, 1), (1, 3, 0, 2), (0, 1, 2, 3))
FAR = [(0, 1), (3, 2)]
NEAR = [(1, 2), (2, 1)]
SECOND = [(0, 2), (3, 1), (1, 0), (2, 3)]
THIRD = [(0, 1), (3, 2), (1, 3), (2, 0)]
MERGE = (0, 1, 2, 0)
KEYS = ((0, 1, 2, 3), (9, 2, 1, 9), (1, 3, 0, 2))
LAST_IN_FRONT = (0, 1, 0, 1)


def gelu(x):
    c = 0.7978845608028654
    half = 0.5 * x
    return half + half * jnp.tanh(x * (c + (c * 0.044715) * (x * x)))


def pair_weights(w_ref):
    zero = jnp.zeros((w_ref.shape[2], w_ref.shape[3]), w_ref.dtype)
    blocks = []
    for j in range(4):
        for d in range(3):
            first = w_ref[j, d] if j < 3 else zero
            second = w_ref[j - 1, d] if j > 0 else zero
            blocks.append(jnp.concatenate([first, second], axis=1))
    return jnp.concatenate(blocks, axis=0)


def odd_row():
    return lax.rem(lax.axis_index("rows"), 2) == 1


def edges_kernel(x_hbm, w_hbm, b_hbm, one_ref, two_ref, w_ref, b_ref, sem):
    rows = x_hbm.shape[2]
    weights = pltpu.make_async_copy(w_hbm, w_ref, sem.at[2])
    bias = pltpu.make_async_copy(b_hbm, b_ref.at[0], sem.at[3])

    def send(near, far):
        a = pltpu.make_async_copy(x_hbm.at[:, :, pl.ds(near, 2)], one_ref, sem.at[0])
        b = pltpu.make_async_copy(x_hbm.at[:, :, pl.ds(far, 2)], two_ref, sem.at[1])
        a.start()
        b.start()
        weights.start()
        bias.start()
        a.wait()
        b.wait()
        weights.wait()
        bias.wait()

    pl.when(odd_row())(functools.partial(send, 0, rows - 2))
    pl.when(jnp.logical_not(odd_row()))(functools.partial(send, rows - 2, 0))


def edges(x, w, b):
    planes, cols, rows, ch = x.shape
    shape = jax.ShapeDtypeStruct((planes, cols, 2, ch), x.dtype)
    return pl.pallas_call(
        edges_kernel,
        out_shape=(
            shape,
            shape,
            jax.ShapeDtypeStruct(w.shape, w.dtype),
            jax.ShapeDtypeStruct((1, ch), F32),
        ),
        in_specs=[HBM] * 3,
        out_specs=(VM,) * 4,
        scratch_shapes=[pltpu.SemaphoreType.DMA((4,))],
        compiler_params=pltpu.CompilerParams(vmem_limit_bytes=8 << 20),
    )(*[pltpu.with_memory_space_constraint(a, pltpu.HBM) for a in (x, w, b)])


def first_conv(xs, w1_ref, bias, c0, cols, emit):
    blocks, wide, ext, ch = xs.shape[1:]
    count = wide - 2
    weights = pair_weights(w1_ref)
    cuts = [count // 2 * i // 2 for i in range(2 + 1)]
    for p, lo, hi in [(p, a, b) for p in range(blocks) for a, b in zip(cuts, cuts[1:])]:
        taps = []
        for j in range(4):
            for d in range(3):
                taps.append(jnp.concatenate([xs[d, p, 2 * g + j] for g in range(lo, hi)], axis=0))
        y = jnp.dot(jnp.concatenate(taps, axis=1), weights, preferred_element_type=F32)
        for c in range(2 * lo, 2 * hi):
            g, o = divmod(c - 2 * lo, 2)
            v = gelu(y[g * ext : (g + 1) * ext, o * ch : (o + 1) * ch] + bias)
            if c == 0:
                v = v * jnp.where(c0 > 0, 1.0, 0.0)
            if c == count - 1:
                v = v * jnp.where(c0 + count - 2 < cols, 1.0, 0.0)
            emit(p, c, v)


def row_masks():
    here = lax.axis_index("rows")
    above = jnp.where(here == 0, 0.0, 1.0)
    below = jnp.where(here == lax.axis_size("rows") - 1, 0.0, 1.0)
    return above, below


def column(c0, c, cols):
    at = c0 - 2 + c
    inside = jnp.logical_and(at >= 0, at < cols)
    return jnp.clip(at, 0, cols - 1), jnp.where(inside, 1.0, 0.0)


def halo_rows(one_ref, two_ref, p, at, odd):
    one = one_ref[p, at].astype(F32)
    two = two_ref[p, at].astype(F32)
    return jnp.where(odd, one, two), jnp.where(odd, two, one)


def second_half(hs, fs, w2_ref, par_ref, out_ref, trans_ref):
    planes, nc, rows, ch = fs.shape
    bias = par_ref[1:2]
    opacity = par_ref[2:3]
    lane = lax.broadcasted_iota(jnp.int32, (rows, ch), 1)
    weights = pair_weights(w2_ref)
    through = jnp.zeros((rows, ch), F32)
    cuts = [nc // 2 * i // 3 for i in range(3 + 1)]
    for lo, hi in zip(cuts, cuts[1:]):
        logits = [jnp.zeros((rows, ch), F32) for _ in range(planes)]
        taps = []
        for j in range(4):
            for d in range(3):
                cells = [hs[d, p, 2 * g + j] for g in range(lo, hi) for p in range(planes)]
                taps.append(jnp.concatenate(cells, axis=0))
        y = jnp.dot(jnp.concatenate(taps, axis=1), weights, preferred_element_type=F32)
        for c in range(2 * lo, 2 * hi):
            g, o = divmod(c - 2 * lo, 2)
            for p in range(planes):
                r0 = (g * planes + p) * rows
                f = gelu(y[r0 : r0 + rows, o * ch : (o + 1) * ch] + bias)
                total = jnp.sum(f * opacity, axis=1, keepdims=True)
                logits[p] = jnp.where(lane == c, total, logits[p])
                fs[p, c] = f
        parts = []
        trans = None
        for p in range(planes):
            alpha = 1.0 / (1.0 + jnp.exp(-(logits[p] + par_ref[3 + p : 4 + p])))
            if p == 0:
                parts.append(alpha)
                trans = 1.0 - alpha
            else:
                parts.append(trans * alpha)
                trans = trans * (1.0 - alpha)
        for c in range(2 * lo, 2 * hi):
            color = sum(parts[p][:, c : c + 1] * fs[p, c] for p in range(planes))
            if trans_ref is None:
                out_ref[c * rows : (c + 1) * rows] = color.astype(BF16)
            else:
                out_ref[c] = color
        mine = jnp.logical_and(lane >= 2 * lo, lane < 2 * hi)
        through = jnp.where(mine, trans, through)
    if trans_ref is None:
        out_ref[nc * rows :] = pack_trans(through, nc)
    else:
        trans_ref[...] = through


def outputs(nc, rows, ch, packed):
    if packed:
        return [jax.ShapeDtypeStruct((nc * rows + rows // folds(nc, rows, ch), ch), BF16)]
    return [jax.ShapeDtypeStruct((nc, rows, ch), F32), jax.ShapeDtypeStruct((rows, ch), F32)]


def call(kernel, args, in_specs, out_shape, scratch):
    return pl.pallas_call(
        kernel,
        out_shape=out_shape,
        in_specs=in_specs,
        out_specs=[VM] * len(out_shape),
        scratch_shapes=scratch,
        compiler_params=pltpu.CompilerParams(vmem_limit_bytes=16 << 20),
        cost_estimate=pl.CostEstimate(flops=5 * 10**9, transcendentals=0, bytes_accessed=10**6),
    )(*args)


def chunk_kernel(pick, packed, x_ref, one_ref, two_ref, w1_ref, w2_ref, par_ref, *refs):
    refs = list(refs)
    out_ref = refs.pop(0)
    trans_ref = None if packed else refs.pop(0)
    f_ref, xs, f2_ref, hs, fs = refs
    planes, cols, rows, ch = x_ref.shape
    nc = fs.shape[1]
    ext = xs.shape[3]
    gap = rows + 8
    c0 = pick() * nc
    odd = odd_row()
    for c in range(nc + 4):
        at, keep = column(c0, c, cols)
        f = f_ref.at[c % f_ref.shape[0]]
        for p in range(planes):
            upper, lower = halo_rows(one_ref, two_ref, p, at, odd)
            r0 = 8 + p * gap
            f[r0 : r0 + rows] = x_ref[p, at].astype(F32) * keep
            f[r0 - 2 : r0] = upper * keep
            f[r0 + rows : r0 + rows + 2] = lower * keep
        for d in range(3):
            xs[d, 0, c] = f[6 + d : 6 + d + ext].astype(BF16)
    above, below = row_masks()

    def emit(_, c, v):
        f2 = f2_ref.at[c]
        f2[...] = v
        for p in range(planes):
            r0 = p * gap
            f2[r0 : r0 + 1] = f2[r0 : r0 + 1] * above
            f2[r0 + rows + 1 : r0 + rows + 2] = f2[r0 + rows + 1 : r0 + rows + 2] * below
            for d in range(3):
                hs[d, p, c] = f2[r0 + d : r0 + d + rows].astype(BF16)

    first_conv(xs, w1_ref, par_ref[0:1], c0, cols, emit)
    second_half(hs, fs, w2_ref, par_ref, out_ref, trans_ref)


def chunk(pick, nc, packed, x, one, two, w1, w2, par):
    planes, cols, rows, ch = x.shape
    ext = -(-((planes - 1) * (rows + 8) + rows + 2) // 16) * 16
    scratch = [
        pltpu.VMEM((4, ext + 16, ch), F32),
        pltpu.VMEM((3, 1, nc + 4, ext, ch), BF16),
        pltpu.VMEM((nc + 2, ext, ch), F32),
        pltpu.VMEM((3, planes, nc + 2, rows, ch), BF16),
        pltpu.VMEM((planes, nc, rows, ch), F32),
    ]
    kernel = functools.partial(chunk_kernel, pick, packed)
    args = (x, one, two, w1, w2, par)
    return call(kernel, args, [VM] * 6, outputs(nc, rows, ch, packed), scratch)


def head_kernel(pick, nc, x_ref, w1_ref, b1_ref, w2_hbm, b2_hbm, ow_hbm, ob_ref, *refs):
    hid_ref, w2_ref, par_ref, f_ref, xs, sem = refs
    planes, cols, rows, ch = x_ref.shape
    pairs = [
        (w2_hbm, w2_ref),
        (b2_hbm, par_ref.at[1]),
        (ow_hbm, par_ref.at[2]),
    ]
    copies = [pltpu.make_async_copy(src, dst, sem.at[i]) for i, (src, dst) in enumerate(pairs)]
    for copy in copies:
        copy.start()
    par_ref[3:] = ob_ref[...]
    c0 = pick() * nc
    for i in range(planes * (nc + 4)):
        p, c = divmod(i, nc + 4)
        at, keep = column(c0, c, cols)
        f = f_ref.at[i % f_ref.shape[0]]
        f[16 : 16 + rows] = x_ref[p, at].astype(F32) * keep
        for d in range(3):
            xs[d, p, c] = f[15 + d : 15 + d + rows].astype(BF16)
    par_ref[0:1] = b1_ref[...]

    def emit(p, c, v):
        hid_ref[p, c, 8 : 8 + rows] = v

    first_conv(xs, w1_ref, b1_ref[...], c0, cols, emit)
    for copy in copies:
        copy.wait()


def head(pick, nc, x, w1, w2, b1, b2, ow, ob):
    planes, cols, rows, ch = x.shape
    args = [pltpu.with_memory_space_constraint(a, pltpu.HBM) for a in (w2, b2, ow)]
    out_shape = [
        jax.ShapeDtypeStruct((planes, nc + 2, rows + 16, ch), F32),
        jax.ShapeDtypeStruct(w2.shape, w2.dtype),
        jax.ShapeDtypeStruct((3 + planes, ch), F32),
    ]
    scratch = [
        pltpu.VMEM((8, rows + 32, ch), F32),
        pltpu.VMEM((3, planes, nc + 4, rows, ch), BF16),
        pltpu.SemaphoreType.DMA((3,)),
    ]
    in_specs = [VM] * 3 + [HBM] * 3 + [VM]
    kernel = functools.partial(head_kernel, pick, nc)
    return call(kernel, (x, w1, b1, *args, ob), in_specs, out_shape, scratch)


def tail_kernel(pick, x_ref, one_ref, two_ref, hid_ref, w1_ref, w2_ref, par_ref, out_ref, *refs):
    f_ref, xs, edge_ref, f2_ref, hs, fs = refs
    planes, cols, rows, ch = x_ref.shape
    nc = fs.shape[1]
    c0 = pick() * nc
    odd = odd_row()
    for i in range(planes * (nc + 4)):
        p, c = divmod(i, nc + 4)
        at, keep = column(c0, c, cols)
        f = f_ref.at[i % f_ref.shape[0]]
        upper, lower = halo_rows(one_ref, two_ref, p, at, odd)
        f[6:8] = upper * keep
        f[8:16] = x_ref[p, at, 0:8].astype(F32) * keep
        f[24:32] = x_ref[p, at, rows - 8 : rows].astype(F32) * keep
        f[32:34] = lower * keep
        for d in range(3):
            both = jnp.concatenate([f[3 + d : 11 + d], f[27 + d : 35 + d]], axis=0)
            xs[d, p, c] = both.astype(BF16)
    above, below = row_masks()

    def emit(p, c, v):
        edge = edge_ref.at[p, c]
        edge[...] = v
        f2 = f2_ref.at[p, c]
        f2[8 : 8 + rows] = hid_ref[p, c, 8 : 8 + rows]
        f2[7:8] = edge[3:4] * above
        f2[8:9] = edge[4:5]
        f2[7 + rows : 8 + rows] = edge[11:12]
        f2[8 + rows : 9 + rows] = edge[12:13] * below
        for d in range(3):
            hs[d, p, c] = f2[7 + d : 7 + d + rows].astype(BF16)

    first_conv(xs, w1_ref, par_ref[0:1], c0, cols, emit)
    second_half(hs, fs, w2_ref, par_ref, out_ref, None)


def tail(pick, nc, x, one, two, hid, w1, w2, par):
    planes, cols, rows, ch = x.shape
    scratch = [
        pltpu.VMEM((8, 40, ch), F32),
        pltpu.VMEM((3, planes, nc + 4, 16, ch), BF16),
        pltpu.VMEM((planes, nc + 2, 16, ch), F32),
        pltpu.VMEM((planes, nc + 2, rows + 16, ch), F32),
        pltpu.VMEM((3, planes, nc + 2, rows, ch), BF16),
        pltpu.VMEM((planes, nc, rows, ch), F32),
    ]
    args = (x, one, two, hid, w1, w2, par)
    kernel = functools.partial(tail_kernel, pick)
    return call(kernel, args, [VM] * 7, outputs(nc, rows, ch, True), scratch)[0]


def lookup(table):
    here = lax.axis_index("depth")
    value = jnp.int32(table[-1])
    for i in range(len(table) - 1):
        value = jnp.where(here == i, table[i], value)
    return value


def folds(nc, rows, ch):
    return min(rows // 16, ch // (2 * nc))


def unpack_trans(ref, nc, rows):
    ch = ref.shape[1]
    fold = folds(nc, rows, ch)
    block = ref[nc * rows :].astype(F32)
    block = block + pltpu.roll(block, ch - nc, axis=1)
    parts = [block] + [pltpu.roll(block, ch - 2 * nc * q, axis=1) for q in range(1, fold)]
    return jnp.concatenate(parts, axis=0)


def pack_trans(trans, nc):
    rows, ch = trans.shape
    fold = folds(nc, rows, ch)
    size = rows // fold
    lane = lax.broadcasted_iota(jnp.int32, trans.shape, 1)
    high = trans.astype(BF16).astype(F32)
    low = pltpu.roll(trans - high, nc, axis=1)
    both = jnp.where(lane < nc, high, jnp.where(lane < 2 * nc, low, 0.0))
    block = both[:size]
    for q in range(1, fold):
        block = block + pltpu.roll(both[q * size : (q + 1) * size], 2 * nc * q, axis=1)
    return block.astype(BF16)


def merge_kernel(own_ref, trans_ref, got_ref, out_ref):
    nc = own_ref.shape[0]
    mine = trans_ref[...]
    rows = own_ref.shape[1]
    theirs = unpack_trans(got_ref, nc, rows)
    role = lookup(MERGE)
    scale_own = jnp.where(role == 1, theirs, 1.0)
    scale_got = jnp.where(role == 2, mine, jnp.where(role == 1, 1.0, 0.0))
    for c in range(nc):
        color = scale_own[:, c : c + 1] * own_ref[c]
        at = slice(c * rows, (c + 1) * rows)
        color = color + scale_got[:, c : c + 1] * got_ref[at].astype(F32)
        out_ref[at] = color.astype(BF16)
    out_ref[nc * rows :] = pack_trans(jnp.where(role == 0, mine, mine * theirs), nc)


def merge(own, trans, got):
    return pl.pallas_call(
        merge_kernel,
        out_shape=jax.ShapeDtypeStruct(got.shape, BF16),
        in_specs=[VM] * 3,
        out_specs=VM,
        compiler_params=pltpu.CompilerParams(vmem_limit_bytes=8 << 20),
        cost_estimate=pl.CostEstimate(flops=10**9, transcendentals=0, bytes_accessed=10**6),
    )(own, trans, got)


def gather_kernel(own_ref, trans_ref, *refs):
    *got_refs, out_ref, out_trans_ref = refs
    nc, rows = own_ref.shape[:2]
    keys = [lookup(table) for table in KEYS]
    trans = [trans_ref[...]] + [unpack_trans(ref, nc, rows) for ref in got_refs]
    scale = []
    through = None
    for k in range(len(trans)):
        w = None
        for m in range(len(trans)):
            if m != k:
                term = jnp.where(keys[m] < keys[k], trans[m], 1.0)
                w = term if w is None else w * term
        scale.append(w)
        term = jnp.where(keys[k] == 9, 1.0, trans[k])
        through = term if through is None else through * term
    for c in range(nc):
        total = scale[0][:, c : c + 1] * own_ref[c]
        for k, ref in enumerate(got_refs):
            at = slice(c * rows, (c + 1) * rows)
            total = total + scale[k + 1][:, c : c + 1] * ref[at].astype(F32)
        out_ref[c] = total
    out_trans_ref[...] = through


def finish_kernel(near_ref, trans_ref, got_ref, out_hbm, out, sem):
    nc, rows = near_ref.shape[:2]
    front = lookup(LAST_IN_FRONT) == 1
    theirs = unpack_trans(got_ref, nc, rows)
    scale_near = jnp.where(front, theirs, 1.0)
    scale_got = jnp.where(front, 1.0, trans_ref[...])
    pieces = sem.shape[0]
    step = nc // pieces
    copies = []
    for i in range(pieces):
        for c in range(i * step, (i + 1) * step):
            got = got_ref[c * rows : (c + 1) * rows].astype(F32)
            out[c] = scale_near[:, c : c + 1] * near_ref[c] + scale_got[:, c : c + 1] * got
        at = pl.ds(i * step, step)
        copies.append(pltpu.make_async_copy(out.at[at], out_hbm.at[at], sem.at[i]))
        copies[-1].start()
    for copy in copies:
        copy.wait()


def combine(own, trans, got):
    color = jax.ShapeDtypeStruct(own.shape, F32)
    near, trans = pl.pallas_call(
        gather_kernel,
        out_shape=[color, jax.ShapeDtypeStruct(trans.shape, F32)],
        in_specs=[VM] * 4,
        out_specs=[VM] * 2,
        compiler_params=pltpu.CompilerParams(vmem_limit_bytes=8 << 20),
        cost_estimate=pl.CostEstimate(flops=10**9, transcendentals=0, bytes_accessed=10**6),
    )(own, trans, *got[:2])
    return pl.pallas_call(
        finish_kernel,
        out_shape=color,
        in_specs=[VM] * 3,
        out_specs=HBM,
        scratch_shapes=[pltpu.VMEM(own.shape, F32), pltpu.SemaphoreType.DMA((4,))],
        compiler_params=pltpu.CompilerParams(vmem_limit_bytes=8 << 20),
    )(near, trans, got[2])


def exchange(value, axis, mask):
    pairs = [(i, i ^ mask) for i in range(lax.axis_size(axis))]
    return lax.ppermute(value, axis, pairs)


def pick_half(array, remaining, bit_set):
    shaped = array.reshape((remaining // 2, 2, -1) + array.shape[1:])
    first_half = shaped[:, 0].reshape((-1,) + array.shape[1:])
    second_half = shaped[:, 1].reshape((-1,) + array.shape[1:])
    keep = jnp.where(bit_set, second_half, first_half)
    other = jnp.where(bit_set, first_half, second_half)
    return (keep, other)


def butterfly(color, trans):
    position = lax.axis_index("depth")
    slabs = lax.axis_size("depth")
    for level in range(slabs.bit_length() - 1):
        remaining = slabs >> level
        bit_set = jnp.right_shift(position, level) % 2 == 1
        keep_color, send_color = pick_half(color, remaining, bit_set)
        keep_trans, send_trans = pick_half(trans, remaining, bit_set)
        got_color = exchange(send_color, "depth", 2**level)
        got_trans = exchange(send_trans, "depth", 2**level)
        color = jnp.where(
            bit_set,
            got_color + got_trans[..., None] * keep_color,
            keep_color + keep_trans[..., None] * got_color,
        )
        trans = keep_trans * got_trans
    return color


def per_device(volume, conv_one, bias_one, conv_two, bias_two, opacity_weight, opacity_bias):
    planes, cols, rows, ch = volume.shape
    slabs = lax.axis_size("depth")
    size = lax.axis_size("rows")
    one, two, w1, b1 = edges(volume, conv_one, bias_one)
    inner = [(i, i + 1) for i in range(1, size - 1, 2)]
    two = lax.ppermute(two, "rows", inner + [(j, i) for i, j in inner])
    one = lax.ppermute(one, "rows", [(i, i ^ 1) for i in range(size)])
    if slabs != 4:
        par = jnp.concatenate(
            [
                jnp.stack([bias_one, bias_two, opacity_weight]),
                jnp.broadcast_to(opacity_bias[:, None], (planes, ch)),
            ]
        )
        args = (16, False, volume, one, two, w1, conv_two, par)
        done = [chunk(functools.partial(jnp.int32, i), *args) for i in range(cols // 16)]
        color = jnp.concatenate([c for c, _ in done])
        trans = jnp.concatenate([jnp.transpose(t[:, :16]) for _, t in done])
        return butterfly(color, trans)
    nc = cols // slabs
    picks = [functools.partial(lookup, [order[slot] for order in PIECE]) for slot in range(4)]
    offsets = jnp.broadcast_to(opacity_bias[:, None], (planes, ch))
    hid, w2, par = head(
        picks[0], nc, volume, w1, conv_two, b1, bias_two, opacity_weight, offsets
    )

    def piece(slot, packed):
        return chunk(picks[slot], nc, packed, volume, one, two, w1, w2, par)

    first = tail(picks[0], nc, volume, one, two, hid, w1, w2, par)
    far = lax.ppermute(first, "depth", FAR)
    near = lax.ppermute(first, "depth", NEAR)
    (second,) = piece(1, True)
    second = lax.ppermute(second, "depth", SECOND)
    third = lax.ppermute(merge(*piece(2, False), far), "depth", THIRD)
    own, trans = piece(3, False)
    return combine(own, trans, [near, second, third])


def solution(mesh):
    in_specs = (P(("grp", "depth"), None, "rows", None), P(), P(), P(), P(), P(), P("depth"))
    out_specs = P(("grp", "depth"), "rows", None)
    return jax.shard_map(
        per_device, mesh=mesh, in_specs=in_specs, out_specs=out_specs, check_vma=False
    )
```
